128 devices in a mesh: outer: 16 (over x, z_hi, core), inner: 8 (over y, z_lo).
Axes of the slice: x: 4, y: 4, z: 4 (z_hi: 2, z_lo: 2; z = z_hi * 2 + z_lo), core: 2. Of those that a mesh axis runs over, the one named last changes fastest.
Arguments:
- tokens: bfloat16 [32768, 2048], P(('outer', 'inner')), may hold values from -16 to 16
- qkv_weight: bfloat16 [2048, 6144], P(None, 'inner'), may hold values from -1 to 1, as said below
- offsets: int32 [16], replicated, may hold values from 0 to 127
Outputs:
- attended: bfloat16 [32768, 2048], P(('outer', 'inner'))
The draws below stay inside these ranges and needn't reach their ends.
Inputs may be any that keep to these rules, and one draw needn't show every extreme that they name: `qkv_weight`: projection entries scaled by the inverse square root of 2048.
All inputs are finite; a program needn't handle non-finite values.
Results may differ from the reference program's by a relative error of at most 0.0067.
Values may be sent and summed in bfloat16 or wider, within the bound.
No kernel may reach another device: no remote copies, remote signals or barrier semaphores. Data moves between devices by JAX's collectives and lax.ppermute only.
A program may use at most 128 MiB of HBM per device.

```python
import math
from functools import reduce
import jax
import jax.numpy as jnp
from jax import lax

D = 2048
HEADS = 16
DH = 128
TOK_DEV = 256
TOKENS = 32768
LEVELS = 7
N_OUTER = 16
N_INNER = 8


def draw_tokens(key, part):
    base_key = jax.random.fold_in(key, 0)
    result = jnp.clip(jax.random.normal(base_key, (TOKENS, D), jnp.float32), -6.0, 6.0)
    return jnp.clip(result, -16.0, 16.0).astype(jnp.bfloat16)


def draw_qkv_weight(key, part):
    first_key = jax.random.fold_in(key, 0)
    spread = D ** (-0.5)
    whole = jnp.clip(jax.random.normal(first_key, (D, HEADS, 3, DH), jnp.float32), -6.0, 6.0) * spread
    return whole.reshape(D, 3 * D).astype(jnp.bfloat16)


def touch_ends(entries, own_key, low, top_value):
    spot = [jax.random.randint(jax.random.fold_in(own_key, axis), (), 0, length) for axis, length in enumerate(entries.shape)]
    widest = entries.shape.index(max(entries.shape))
    next_to = spot[:widest] + [(spot[widest] + 1) % entries.shape[widest]] + spot[widest + 1:]
    return entries.at[tuple(spot)].set(low).at[tuple(next_to)].set(top_value)


def setup_inputs(seed: int = 0) -> dict:
    key_list = jax.random.split(jax.random.key(seed), 4)
    return {
        "tokens": draw_tokens(jax.random.fold_in(key_list[3], 71), 0),
        "qkv_weight": draw_qkv_weight(jax.random.fold_in(key_list[3], 71), 0),
        "offsets": touch_ends(jax.random.randint(key_list[2], (HEADS,), 0, N_OUTER * N_INNER), jax.random.fold_in(key_list[2], 1), 0, (N_OUTER * N_INNER) - 1).astype(jnp.int32),
    }


def select_rows(source, stride, offsets):
    row_count = source.shape[0]
    shaped = source.reshape((row_count // stride, stride) + source.shape[1:])
    wanted = jnp.arange(stride, dtype=jnp.int32)[:, None] == (offsets % stride)[None, :]
    masked = jnp.where(wanted[None, :, :, None], shaped, jnp.zeros((), source.dtype))
    return lax.optimization_barrier(jnp.sum(masked, axis=1))

def attend(queries, keys_values, inv_root):
    key_part = keys_values[:, :, :DH].astype(jnp.float32)
    value_part = keys_values[:, :, DH:].astype(jnp.float32)
    raw_scores = jnp.einsum('qhd,khd->hqk', queries.astype(jnp.float32), key_part)
    scores = raw_scores * inv_root
    row_top = lax.optimization_barrier(jnp.max(scores, axis=2))
    exponent = jnp.exp(scores - row_top[:, :, None])
    row_total = lax.optimization_barrier(jnp.sum(exponent, axis=2))
    weights = lax.optimization_barrier(exponent.astype(jnp.bfloat16))
    row_mixed = jnp.einsum('hqk,khd->hqd', weights.astype(jnp.float32), value_part)
    return (row_top, row_total, row_mixed)

def reference(tokens, qkv_weight, offsets):
    devices = N_OUTER * N_INNER
    inv_root = 1.0 / math.sqrt(DH)
    blocks = tokens.reshape(devices, TOK_DEV, D)
    projected = lax.map(lambda block_rows: jnp.dot(block_rows, qkv_weight, preferred_element_type=jnp.float32).astype(jnp.bfloat16), blocks)
    sections = projected.reshape(TOKENS, HEADS, 3, DH)
    queries = sections[:, :, 0]
    key_value = sections[:, :, 1:].reshape(TOKENS, HEADS, 2 * DH)
    chosen_sets = []
    for level_index in range(LEVELS + 1):
        stride = 2 ** level_index
        picked = select_rows(key_value, stride, offsets)
        chosen_sets.append(picked.reshape(devices // stride, TOK_DEV, HEADS, 2 * DH))

    def device_rows(device_index):
        own_queries = lax.dynamic_slice_in_dim(queries, device_index * TOK_DEV, TOK_DEV, 0)
        level_tops = []
        totals = []
        level_mixes = []
        covers = []
        for level_index in range(LEVELS + 1):
            stride = 2 ** level_index
            level_queries = select_rows(own_queries, stride, offsets)
            segment = lax.dynamic_index_in_dim(chosen_sets[level_index], device_index // stride, 0, keepdims=False)
            row_top, row_total, row_mixed = attend(level_queries, segment, inv_root)
            cover = jnp.arange(stride, dtype=jnp.int32)[None, None, :] == (offsets % stride)[:, None, None]
            cover = jnp.broadcast_to(cover, (HEADS, TOK_DEV // stride, stride))
            covers.append(cover.reshape(HEADS, TOK_DEV))
            level_tops.append(jnp.where(cover, row_top[:, :, None], -1e+30).reshape(HEADS, TOK_DEV))
            totals.append(jnp.where(cover, row_total[:, :, None], 0.0).reshape(HEADS, TOK_DEV))
            level_mixes.append(jnp.where(cover[:, :, :, None], row_mixed[:, :, None, :], 0.0).reshape(HEADS, TOK_DEV, DH))
        overall_top = reduce(jnp.maximum, level_tops)
        numerator = jnp.zeros((HEADS, TOK_DEV, DH), jnp.float32)
        denominator = jnp.zeros((HEADS, TOK_DEV), jnp.float32)
        for level_index in range(LEVELS + 1):
            factor = jnp.where(covers[level_index], jnp.exp(level_tops[level_index] - overall_top), 0.0)
            denominator = denominator + factor * totals[level_index]
            numerator = numerator + factor[:, :, None] * level_mixes[level_index]
        result = (numerator / denominator[:, :, None]).astype(jnp.bfloat16)
        return jnp.transpose(result, (1, 0, 2)).reshape(TOK_DEV, D)
    rows_out = lax.map(device_rows, jnp.arange(devices, dtype=jnp.int32))
    return rows_out.reshape(TOKENS, D)
```

```python
import math

import jax
import jax.numpy as jnp
from jax import lax
from jax.experimental import pallas as pl
from jax.experimental.pallas import tpu as pltpu
from jax.sharding import PartitionSpec as P


HEADS = 16
DH = 128
ROWS = 256
DEEP = 32
SLABS = 4
SLOTS = 4
BF = jnp.bfloat16
F32 = jnp.float32
VMEM_BYTES = 56 * 1024 * 1024


def flipped(value, o_mask, i_mask):
    inner = lax.axis_size("inner")
    count = inner * lax.axis_size("outer")
    mask = o_mask * inner + i_mask
    return lax.ppermute(value, ("outer", "inner"), [(f, f ^ mask) for f in range(count)])


def head_of(place_ref, m, slot):
    shard = place_ref[0] ^ m ^ (6 * (slot >> 1))
    return 2 * shard + ((slot & 1) ^ place_ref[1])


def position_of(row, offset):
    index = row >> 1
    reverse = jnp.zeros_like(index)
    for bit in range(7):
        reverse = reverse | (((index >> bit) & 1) << (6 - bit))
    return ((row & 1) << 7) | (reverse ^ (offset & 127))


def to_order(offset):
    row = lax.broadcasted_iota(jnp.int32, (ROWS, ROWS), 0)
    column = lax.broadcasted_iota(jnp.int32, (ROWS, ROWS), 1)
    return jnp.where(position_of(row, offset) == column, 1.0, 0.0).astype(BF)


def from_order(offset, count):
    row = lax.broadcasted_iota(jnp.int32, (ROWS, count), 0)
    column = lax.broadcasted_iota(jnp.int32, (ROWS, count), 1)
    return jnp.where(position_of(column, offset) == row, 1.0, 0.0).astype(BF)


def project_body(base, place_ref, offsets_ref, x0, x1, x2, x3, w_ref, *rest):
    qkv_ref, deep_q_ref, deep_kv_ref, spread = rest[-4:]
    offset = offsets_ref[head_of(place_ref, 0, base + pl.program_id(0))]
    order = to_order(offset)
    for m, x_ref in enumerate((x0, x1, x2, x3)):
        rows = jnp.dot(x_ref[...], w_ref[...], preferred_element_type=F32).astype(BF)
        rows = jnp.dot(order, rows, preferred_element_type=F32)
        qkv_ref[0, m] = rows.astype(BF)
        for part in range(3):
            spread[part, pl.ds(m, DEEP, stride=SLABS), :] = rows[:DEEP, part * DH : (part + 1) * DH]
    deep_q_ref[0] = spread[0].astype(BF)
    deep_kv_ref[0, :, :DH] = spread[1].astype(BF)
    deep_kv_ref[0, :, DH:] = spread[2].astype(BF)


def project(place, offsets, slabs, weight, base, heads, core_order, carried):
    shapes = (
        jax.ShapeDtypeStruct((SLOTS, SLABS, ROWS, 3 * DH), BF),
        jax.ShapeDtypeStruct((SLOTS, SLABS * DEEP, DH), BF),
        jax.ShapeDtypeStruct((SLOTS, SLABS * DEEP, 2 * DH), BF),
    )
    depth = weight.shape[0]

    def weight_block(j, place_ref, offsets_ref):
        return (0, place_ref[1] ^ j if core_order else j)

    carried = () if carried is None else tuple(carried)
    return pl.pallas_call(
        lambda *refs: project_body(base, *refs),
        out_shape=shapes,
        grid_spec=pltpu.PrefetchScalarGridSpec(
            num_scalar_prefetch=2,
            grid=(heads,),
            in_specs=[pl.BlockSpec((ROWS, depth), lambda j, *_: (0, 0)) for _ in slabs]
            + [pl.BlockSpec((depth, 3 * DH), weight_block)]
            + [pl.BlockSpec(memory_space=pl.ANY) for _ in carried],
            out_specs=[
                pl.BlockSpec((1, SLABS, ROWS, 3 * DH), lambda j, *_: (base + j, 0, 0, 0)),
                pl.BlockSpec((1, SLABS * DEEP, DH), lambda j, *_: (base + j, 0, 0)),
                pl.BlockSpec((1, SLABS * DEEP, 2 * DH), lambda j, *_: (base + j, 0, 0)),
            ],
            scratch_shapes=[pltpu.VMEM((3, SLABS * DEEP, DH), F32)],
        ),
        input_output_aliases={7 + k: k for k in range(len(carried))},
        compiler_params=pltpu.CompilerParams(vmem_limit_bytes=VMEM_BYTES),
        cost_estimate=pl.CostEstimate(
            flops=heads * SLABS * 2 * ROWS * 3 * DH * (depth + ROWS),
            bytes_accessed=SLABS * ROWS * depth * 2 + heads * depth * 3 * DH * 2,
            transcendentals=0,
        ),
        name="project",
    )(place, offsets, *slabs, weight, *carried)


def attend(q, k, v):
    scores = lax.dot_general(q, k, (((1,), (1,)), ((), ())), preferred_element_type=F32)
    scores = scores * (1.0 / math.sqrt(DH))
    top = jnp.max(scores, axis=1, keepdims=True)
    exponent = jnp.exp(scores - top)
    total = jnp.sum(exponent, axis=1, keepdims=True)
    mixed = jnp.dot(exponent.astype(BF), v, preferred_element_type=F32)
    return top, total, mixed


def merge(fine, coarse):
    top = jnp.maximum(fine[0], coarse[0])
    fine_scale = jnp.exp(fine[0] - top)
    coarse_scale = jnp.exp(coarse[0] - top)
    return (
        top,
        fine[1] * fine_scale + coarse[1] * coarse_scale,
        fine[2] * fine_scale + coarse[2] * coarse_scale,
    )


def near_body(place_ref, offsets_ref, qkv_ref, u0, u1, u2, u3, state_ref):
    offset = offsets_ref[head_of(place_ref, 0, pl.program_id(0))]
    back = from_order(offset, ROWS)

    def rows_of(members, count):
        parts = []
        for part in range(3):
            pieces = [qkv_ref[0, m, :count, part * DH : (part + 1) * DH] for m in members]
            parts.append(pieces[0] if len(pieces) == 1 else jnp.concatenate(pieces, axis=0))
        return parts

    second = attend(*rows_of(range(SLABS), ROWS // 4))
    for pair in range(2):
        first = attend(*rows_of((2 * pair, 2 * pair + 1), ROWS // 2))
        for side in range(2):
            m = 2 * pair + side
            dense = attend(*rows_of((m,), ROWS))
            half = merge(
                tuple(value[: ROWS // 2] for value in dense),
                tuple(value[side * ROWS // 2 : (side + 1) * ROWS // 2] for value in first),
            )
            quarter = merge(
                tuple(value[: ROWS // 4] for value in half),
                tuple(value[m * ROWS // 4 : (m + 1) * ROWS // 4] for value in second),
            )
            for part in range(3):
                state_ref[0, part, pl.ds(m, DEEP, stride=SLABS), :] = jnp.broadcast_to(
                    quarter[part][:DEEP], (DEEP, DH)
                )
            done = jnp.concatenate(
                [
                    jnp.zeros((DEEP, DH), F32),
                    quarter[2][DEEP:] / quarter[1][DEEP:],
                    half[2][ROWS // 4 :] / half[1][ROWS // 4 :],
                    dense[2][ROWS // 2 :] / dense[1][ROWS // 2 :],
                ],
                axis=0,
            ).astype(BF)
            (u0, u1, u2, u3)[m][0] = jnp.dot(back, done, preferred_element_type=F32).astype(BF)


def near(place, offsets, qkv):
    return pl.pallas_call(
        near_body,
        out_shape=tuple(jax.ShapeDtypeStruct((SLOTS, ROWS, DH), BF) for _ in range(SLABS))
        + (jax.ShapeDtypeStruct((SLOTS, 3, SLABS * DEEP, DH), F32),),
        grid_spec=pltpu.PrefetchScalarGridSpec(
            num_scalar_prefetch=2,
            grid=(SLOTS,),
            in_specs=[pl.BlockSpec((1, SLABS, ROWS, 3 * DH), lambda j, *_: (j, 0, 0, 0))],
            out_specs=[pl.BlockSpec((1, ROWS, DH), lambda j, *_: (j, 0, 0)) for _ in range(SLABS)]
            + [pl.BlockSpec((1, 3, SLABS * DEEP, DH), lambda j, *_: (j, 0, 0, 0))],
        ),
        compiler_params=pltpu.CompilerParams(vmem_limit_bytes=VMEM_BYTES),
        cost_estimate=pl.CostEstimate(
            flops=SLOTS * 7 * 4 * ROWS * ROWS * DH,
            bytes_accessed=SLOTS * SLABS * ROWS * 4 * DH * 2,
            transcendentals=SLOTS * 7 * ROWS * ROWS,
        ),
        name="near",
    )(place, offsets, qkv)


def far_body(q_ref, state_ref, *refs):
    pairs = refs[:10]
    outs = refs[10:14]
    spread = refs[14]
    combined = tuple(state_ref[0, part] for part in range(3))
    combined = (combined[0][:, :1], combined[1][:, :1], combined[2])
    tails = []
    for level in range(5):
        rows = SLABS * DEEP >> level
        kept_ref, other_ref = pairs[2 * level], pairs[2 * level + 1]
        keys = jnp.concatenate([kept_ref[0, :, :DH], other_ref[0, :, :DH]], axis=0)
        values = jnp.concatenate([kept_ref[0, :, DH:], other_ref[0, :, DH:]], axis=0)
        found = attend(q_ref[0, : max(rows, 16), :], keys, values)
        combined = merge(combined, tuple(value[:rows] for value in found))
        half = rows // 2 if level < 4 else 0
        tails.append(combined[2][half:] / combined[1][half:])
        combined = tuple(value[:half] for value in combined)
    spread[...] = jnp.concatenate(tails[::-1], axis=0)
    for m in range(SLABS):
        outs[m][0] = spread[pl.ds(m, DEEP, stride=SLABS), :].astype(BF)


def far(deep_q, state, pairs):
    rows = SLABS * DEEP
    return pl.pallas_call(
        far_body,
        out_shape=tuple(jax.ShapeDtypeStruct((SLOTS, DEEP, DH), BF) for _ in range(SLABS)),
        grid=(SLOTS,),
        in_specs=[
            pl.BlockSpec((1, rows, DH), lambda j: (j, 0, 0)),
            pl.BlockSpec((1, 3, rows, DH), lambda j: (j, 0, 0, 0)),
        ]
        + [pl.BlockSpec((1, rows, 2 * DH), lambda j: (j, 0, 0)) for _ in pairs],
        out_specs=[pl.BlockSpec((1, DEEP, DH), lambda j: (j, 0, 0)) for _ in range(SLABS)],
        scratch_shapes=[pltpu.VMEM((rows, DH), F32)],
        compiler_params=pltpu.CompilerParams(vmem_limit_bytes=VMEM_BYTES),
        cost_estimate=pl.CostEstimate(
            flops=SLOTS * 2 * 4 * rows * ROWS * DH,
            bytes_accessed=SLOTS * rows * 10 * 2 * DH * 2,
            transcendentals=SLOTS * 2 * rows * ROWS,
        ),
        name="far",
    )(deep_q, state, *pairs)


def place_body(place_ref, offsets_ref, *refs):
    bulk, deep, out_ref = refs[:4], refs[4:8], refs[8]
    for m in range(SLABS):
        for slot in range(SLOTS):
            head = head_of(place_ref, m, slot)
            back = from_order(offsets_ref[head], DEEP)
            rows = jnp.dot(back, deep[m][slot], preferred_element_type=F32)
            column = pl.multiple_of(head * DH, DH)
            out_ref[:, pl.ds(column, DH)] = (bulk[m][slot].astype(F32) + rows).astype(BF)


def placed_heads(place, offsets, bulk, deep):
    whole = pl.BlockSpec(memory_space=pltpu.VMEM)
    scalars = pl.BlockSpec(memory_space=pltpu.SMEM)
    return pl.pallas_call(
        place_body,
        out_shape=jax.ShapeDtypeStruct((ROWS, HEADS * DH), BF),
        in_specs=[scalars, scalars] + [whole] * 8,
        out_specs=whole,
        compiler_params=pltpu.CompilerParams(vmem_limit_bytes=VMEM_BYTES),
        cost_estimate=pl.CostEstimate(
            flops=HEADS * 2 * ROWS * DEEP * DH,
            bytes_accessed=2 * ROWS * HEADS * DH * 2,
            transcendentals=0,
        ),
        name="place",
    )(place, offsets, *bulk, *deep)


def halves(value, pieces):
    heads, rows, width = value.shape
    part = rows // pieces
    return [value[:, k * part : k * part + part // 2] for k in range(pieces)]


def swap_slots(value):
    return jnp.concatenate([value[2:], value[:2]], axis=0)


def swap_cores(value):
    return jnp.concatenate([value[1:2], value[0:1], value[3:4], value[2:3]], axis=0)


def shards(tokens, qkv_weight, offsets):
    inner = lax.axis_index("inner").astype(jnp.int32)
    core = lax.axis_index("outer").astype(jnp.int32) & 1
    place = jnp.stack([inner, core])
    depth = qkv_weight.shape[0]

    sent = lax.dynamic_slice(qkv_weight, (0, core * 3 * DH), (depth, 3 * DH))
    weight_got = flipped(sent, 0, 6)
    slab_z = flipped(tokens, 0, 1)
    slab_y = flipped(tokens, 0, 2)
    slab_d = flipped(tokens, 0, 3)
    weight_rest = flipped(weight_got, 1, 0)
    slabs = (tokens, slab_z, slab_y, slab_d)

    carried = project(place, offsets, slabs, qkv_weight, 0, 2, True, None)
    carried = project(place, offsets, slabs, weight_got, 2, 1, False, carried)
    qkv, deep_q, deep_kv = project(place, offsets, slabs, weight_rest, 3, 1, False, carried)

    other = flipped(swap_slots(deep_kv), 0, 4 | 2)
    pairs = [deep_kv, other]
    kept, pieces = deep_kv, 1
    for level in range(4):
        kept = jnp.concatenate(halves(kept, pieces) + halves(other, pieces), axis=1)
        pieces *= 2
        other = flipped(swap_cores(kept) if level == 0 else kept, 1 << level, 0)
        pairs += [kept, other]

    *bulk, state = near(place, offsets, qkv)
    bulk = [bulk[0]] + [flipped(bulk[m], 0, m) for m in range(1, SLABS)]
    deep = far(deep_q, state, pairs)
    deep = [deep[0]] + [flipped(deep[m], 0, m) for m in range(1, SLABS)]
    return placed_heads(place, offsets, bulk, deep)


def solution(mesh):
    placed = (P(("outer", "inner"), None), P(None, "inner"), P())
    return jax.shard_map(
        shards, mesh=mesh, in_specs=placed, out_specs=P(("outer", "inner"), None), check_vma=False
    )
```

```python
import math

import jax
import jax.numpy as jnp
from jax import lax
from jax.experimental import pallas as pl
from jax.experimental.pallas import tpu as pltpu
from jax.sharding import PartitionSpec as P


HEADS = 16
DH = 128
ROWS = 256
DEEP = 32
SLABS = 4
SLOTS = 4
DROWS = SLABS * DEEP
BF = jnp.bfloat16
F32 = jnp.float32
I32 = jnp.int32
VMEM_BYTES = 24 * 1024 * 1024
LOW = -1e30


def flipped(value, o_mask, i_mask):
    inner = lax.axis_size("inner")
    count = inner * lax.axis_size("outer")
    mask = o_mask * inner + i_mask
    return lax.ppermute(value, ("outer", "inner"), [(f, f ^ mask) for f in range(count)])


def head_of(place_ref, m, slot):
    shard = place_ref[0] ^ m ^ (6 * (slot >> 1))
    return 2 * shard + (slot & 1)


def position_of(row, offset):
    index = row >> 1
    reverse = jnp.zeros_like(index)
    for bit in range(7):
        reverse = reverse | (((index >> bit) & 1) << (6 - bit))
    return ((row & 1) << 7) | (reverse ^ (offset & 127))


def to_order(offset):
    row = lax.broadcasted_iota(I32, (ROWS, 1), 0)
    column = lax.broadcasted_iota(I32, (ROWS, ROWS), 1)
    return jnp.where(position_of(row, offset) == column, 1.0, 0.0).astype(BF)


def from_order(offset, count):
    row = lax.broadcasted_iota(I32, (ROWS, count), 0)
    column = lax.broadcasted_iota(I32, (1, count), 1)
    return jnp.where(position_of(column, offset) == row, 1.0, 0.0).astype(BF)


def project_body(groups, n_x, n_w, first_slot, last_deep, *refs):
    place_ref, offsets_ref = refs[:2]
    xs, ws = refs[2 : 2 + n_x], refs[2 + n_x : 2 + n_x + n_w]
    qkv_ref, orders = refs[-2 - 2 * last_deep], refs[-1]
    for k in range(2):
        orders[k] = to_order(offsets_ref[head_of(place_ref, 0, first_slot + k)])
    chunk = ws[0].shape[0]
    for members in groups:
        total = None
        for index, w_ref in enumerate(ws):
            if n_w == 1:
                columns = slice(None)
            else:
                per_core = n_w // 2
                start = (place_ref[1] ^ (index // per_core)) * per_core + index % per_core
                columns = pl.ds(pl.multiple_of(start * chunk, chunk), chunk)
            rows = [xs[piece][:, columns] for _, pieces in members for piece in pieces]
            rows = rows[0] if len(rows) == 1 else jnp.concatenate(rows, axis=0)
            product = jnp.dot(rows, w_ref[...], preferred_element_type=F32)
            total = product if total is None else total + product
        total = total.astype(BF)
        for number, (m, _) in enumerate(members):
            for k in range(2):
                found = total[number * ROWS : (number + 1) * ROWS, k * 3 * DH : (k + 1) * 3 * DH]
                found = jnp.dot(orders[k], found, preferred_element_type=F32)
                qkv_ref[m, first_slot + k] = found.astype(BF)


def spread_body(qkv_ref, deep_q_ref, deep_kv_ref, spread):
    for slot in range(SLOTS):
        for part in range(3):
            for m in range(SLABS):
                piece = qkv_ref[m, slot, :DEEP, part * DH : (part + 1) * DH].astype(F32)
                spread[slot, part, pl.ds(m, DEEP, stride=SLABS), :] = piece
        deep_q_ref[slot] = spread[slot, 0].astype(BF)
        deep_kv_ref[slot, :, :DH] = spread[slot, 1].astype(BF)
        deep_kv_ref[slot, :, DH:] = spread[slot, 2].astype(BF)


def project(place, offsets, xs, ws, groups, first_slot, carried, last_deep):
    whole = pl.BlockSpec(memory_space=pltpu.VMEM)
    scalars = pl.BlockSpec(memory_space=pltpu.SMEM)
    out_shape = [jax.ShapeDtypeStruct((SLABS, SLOTS, ROWS, 3 * DH), BF)]
    scratch = [pltpu.VMEM((2, ROWS, ROWS), BF)]
    if last_deep:
        out_shape += [
            jax.ShapeDtypeStruct((SLOTS, DROWS, DH), BF),
            jax.ShapeDtypeStruct((SLOTS, DROWS, 2 * DH), BF),
        ]
        scratch.append(pltpu.VMEM((SLOTS, 3, DROWS, DH), F32))
    extra = [] if carried is None else [carried]

    def body(*refs):
        if not last_deep:
            project_body(groups, len(xs), len(ws), first_slot, 0, *refs)
            return
        *front, qkv_ref, deep_q_ref, deep_kv_ref, orders, spread = refs
        project_body(groups, len(xs), len(ws), first_slot, 0, *front, qkv_ref, orders)
        spread_body(qkv_ref, deep_q_ref, deep_kv_ref, spread)

    slabs = sum(len(members) for members in groups)
    depth, width = xs[0].shape[1], ws[0].shape[1]
    return pl.pallas_call(
        body,
        out_shape=out_shape,
        in_specs=[scalars, scalars] + [whole] * (len(xs) + len(ws) + len(extra)),
        out_specs=[whole] * len(out_shape),
        scratch_shapes=scratch,
        input_output_aliases={2 + len(xs) + len(ws): 0} if extra else {},
        compiler_params=pltpu.CompilerParams(vmem_limit_bytes=VMEM_BYTES),
        cost_estimate=pl.CostEstimate(
            flops=slabs * 2 * ROWS * width * (depth + ROWS),
            bytes_accessed=slabs * ROWS * depth * 2 + depth * width * 2,
            transcendentals=0,
        ),
        name="project",
    )(place, offsets, *xs, *ws, *extra)


def scores_of(q, k):
    scores = lax.dot_general(q, k, (((1,), (1,)), ((), ())), preferred_element_type=F32)
    return scores * (1.0 / math.sqrt(DH))


def weigh(scores, top, v, count):
    exponent = jnp.exp(scores - top)
    if count is not None:
        exponent = exponent * count
    total = jnp.sum(exponent, axis=1, keepdims=True)
    return total, jnp.dot(exponent.astype(BF), v, preferred_element_type=F32)


def near_body(base, heads, n_extra, place_ref, offsets_ref, qkv_ref, *refs):
    *outs, state_ref = refs[n_extra:]

    @pl.loop(0, heads)
    def _(j):
        slot = base + j
        back = from_order(offsets_ref[head_of(place_ref, 0, slot)], ROWS)

        def rows_of(members, count):
            parts = []
            for part in range(3):
                pieces = [qkv_ref[m, slot, :count, part * DH : (part + 1) * DH] for m in members]
                parts.append(pieces[0] if len(pieces) == 1 else jnp.concatenate(pieces, axis=0))
            return parts

        sets = [rows_of((m,), ROWS) for m in range(SLABS)]
        sets += [rows_of((0, 1), ROWS // 2), rows_of((2, 3), ROWS // 2), rows_of(range(SLABS), ROWS // 4)]
        scores = [scores_of(q, k) for q, k, _ in sets]
        wide = [jnp.maximum(score[:, :DH], score[:, DH:]) for score in scores]
        tops = []
        for m in range(SLABS):
            pair = wide[4 + m // 2][m % 2 * 128 : m % 2 * 128 + 128]
            four = wide[6][m * 64 : m * 64 + 64]
            first = jnp.maximum(wide[m][:64], jnp.maximum(pair[:64], four))
            second = jnp.maximum(wide[m][64:128], pair[64:])
            top = jnp.concatenate([first, second, wide[m][128:]], axis=0)
            tops.append(jnp.max(top, axis=1, keepdims=True))
        tops += [jnp.concatenate([top[:128] for top in tops[2 * k : 2 * k + 2]], axis=0) for k in range(2)]
        tops.append(jnp.concatenate([top[:64] for top in tops[:SLABS]], axis=0))
        found = [weigh(scores[k], tops[k], sets[k][2], None) for k in range(7)]
        for m in range(SLABS):
            sums = []
            for part in range(2):
                dense, four = found[m][part], found[6][part][m * 64 : m * 64 + 64]
                pair = found[4 + m // 2][part][m % 2 * 128 : m % 2 * 128 + 128]
                sums.append((dense[:64] + pair[:64] + four, dense[64:128] + pair[64:], dense[128:]))
            for part, value in enumerate((tops[m], sums[0][0], sums[1][0])):
                state_ref[slot, part, pl.ds(m, DEEP, stride=SLABS), :] = jnp.broadcast_to(
                    value[:DEEP], (DEEP, DH)
                )
            done = jnp.concatenate(
                [jnp.zeros((DEEP, DH), F32), sums[1][0][DEEP:] / sums[0][0][DEEP:]]
                + [sums[1][k] / sums[0][k] for k in (1, 2)],
                axis=0,
            ).astype(BF)
            outs[m][slot] = jnp.dot(back, done, preferred_element_type=F32).astype(BF)


def near(place, offsets, qkv, base, heads, carried):
    whole = pl.BlockSpec(memory_space=pltpu.VMEM)
    scalars = pl.BlockSpec(memory_space=pltpu.SMEM)
    return pl.pallas_call(
        lambda *refs: near_body(base, heads, len(carried), *refs),
        out_shape=tuple(jax.ShapeDtypeStruct((SLOTS, ROWS, DH), BF) for _ in range(SLABS))
        + (jax.ShapeDtypeStruct((SLOTS, 3, DROWS, DH), F32),),
        in_specs=[scalars, scalars] + [whole] * (1 + len(carried)),
        out_specs=[whole] * 5,
        input_output_aliases={3 + k: k for k in range(len(carried))},
        compiler_params=pltpu.CompilerParams(vmem_limit_bytes=VMEM_BYTES),
        cost_estimate=pl.CostEstimate(
            flops=heads * 7 * 4 * ROWS * ROWS * DH,
            bytes_accessed=heads * SLABS * ROWS * 4 * DH * 2,
            transcendentals=heads * 7 * ROWS * ROWS,
        ),
        name="near",
    )(place, offsets, qkv, *carried)


def level_of(row):
    level = jnp.full_like(row, 3)
    for deeper in range(4):
        level = level + jnp.where(row < (64 >> deeper), 1, 0)
    return level


def count_of(rows, pieces, piece, lowest):
    query = level_of(lax.broadcasted_iota(I32, (rows, 1), 0))
    key = level_of(lax.broadcasted_iota(I32, (1, pieces * piece), 1) & (piece - 1))
    return jnp.maximum(jnp.minimum(query, key) - (lowest - 1), 0).astype(F32)


def join(state, scores, counts, values):
    old_top, old_total, old_mixed = state
    masked = [jnp.where(count > 0, score, LOW) for score, count in zip(scores, counts)]
    top = old_top
    for score in masked:
        top = jnp.maximum(top, jnp.max(score, axis=1, keepdims=True))
    scale = jnp.exp(old_top - top)
    total, mixed = old_total * scale, old_mixed * scale
    for score, count, value in zip(masked, counts, values):
        more_total, more_mixed = weigh(score, top, value, count)
        total, mixed = total + more_total, mixed + more_mixed
    return top, total, mixed


def middle_body(q_ref, near_ref, own_ref, other_ref, core_ref, done_ref, state_ref):
    for slot in range(SLOTS):
        state = tuple(near_ref[slot, part] for part in range(3))
        state = (state[0][:, :1], state[1][:, :1], state[2])
        keys = [own_ref[slot, :, :DH], other_ref[slot, :, :DH], core_ref[slot, :, :DH]]
        values = [own_ref[slot, :, DH:], other_ref[slot, :, DH:], core_ref[slot, :, DH:]]
        scores = [scores_of(q_ref[slot], key) for key in keys]
        counts = [count_of(DROWS, 1, DROWS, 3), count_of(DROWS, 1, DROWS, 3), count_of(DROWS, 2, 64, 4)]
        top, total, mixed = join(state, scores, counts, values)
        done_ref[slot] = mixed[DEEP:] / total[DEEP:]
        for part, value in enumerate((top, total, mixed)):
            state_ref[slot, part] = jnp.broadcast_to(value[:DEEP], (DEEP, DH))


def middle(deep_q, state, own, other, core):
    whole = pl.BlockSpec(memory_space=pltpu.VMEM)
    return pl.pallas_call(
        middle_body,
        out_shape=(
            jax.ShapeDtypeStruct((SLOTS, DROWS - DEEP, DH), F32),
            jax.ShapeDtypeStruct((SLOTS, 3, DEEP, DH), F32),
        ),
        in_specs=[whole] * 5,
        out_specs=[whole] * 2,
        compiler_params=pltpu.CompilerParams(vmem_limit_bytes=VMEM_BYTES),
        cost_estimate=pl.CostEstimate(
            flops=SLOTS * 4 * DROWS * 3 * DROWS * DH,
            bytes_accessed=SLOTS * DROWS * 10 * DH * 2,
            transcendentals=SLOTS * DROWS * 3 * DROWS,
        ),
        name="middle",
    )(deep_q, state, own, other, core)


def far_body(place_ref, q_ref, state_ref, done_ref, mine5, mine6, mine7, their5, their6, their7, *rest):
    outs, spread = rest[:SLABS], rest[SLABS]
    core = place_ref[1]
    for slot in range(SLOTS):
        state = tuple(state_ref[slot, part] for part in range(3))
        state = (state[0][:, :1], state[1][:, :1], state[2])
        keys, values = [], []
        for mine, their in ((mine5, their5), (mine6, their6), (mine7, their7)):
            found = jnp.where(core == slot % 2, mine[slot // 2], their[slot // 2])
            keys.append(found[:, :DH])
            values.append(found[:, DH:])
        scores = [scores_of(q_ref[slot, :DEEP], key) for key in keys]
        counts = [count_of(DEEP, 4, 32, 5), count_of(DEEP, 8, 16, 6), count_of(DEEP, 16, 8, 7)]
        _, total, mixed = join(state, scores, counts, values)
        spread[slot, :DEEP] = mixed / total
        spread[slot, DEEP:] = done_ref[slot]
        for m in range(SLABS):
            outs[m][slot] = spread[slot, pl.ds(m, DEEP, stride=SLABS), :].astype(BF)


def far(place, deep_q, state, done, mine, their):
    whole = pl.BlockSpec(memory_space=pltpu.VMEM)
    return pl.pallas_call(
        far_body,
        out_shape=tuple(jax.ShapeDtypeStruct((SLOTS, DEEP, DH), BF) for _ in range(SLABS)),
        in_specs=[pl.BlockSpec(memory_space=pltpu.SMEM)] + [whole] * 9,
        out_specs=[whole] * SLABS,
        scratch_shapes=[pltpu.VMEM((SLOTS, DROWS, DH), F32)],
        compiler_params=pltpu.CompilerParams(vmem_limit_bytes=VMEM_BYTES),
        cost_estimate=pl.CostEstimate(
            flops=SLOTS * 4 * DEEP * 3 * DROWS * DH,
            bytes_accessed=SLOTS * DROWS * 8 * DH * 2,
            transcendentals=SLOTS * DEEP * 3 * DROWS,
        ),
        name="far",
    )(place, deep_q, state, done, *mine, *their)


def place_body(place_ref, offsets_ref, *refs):
    bulk, deep, out_ref = refs[:4], refs[4:8], refs[8]
    for m in range(SLABS):
        for slot in range(SLOTS):
            head = head_of(place_ref, m, slot)
            back = from_order(offsets_ref[head], DEEP)
            rows = jnp.dot(back, deep[m][slot], preferred_element_type=F32)
            column = pl.multiple_of(head * DH, DH)
            early = bulk[m][slot]
            out_ref[:, pl.ds(column, DH)] = (early.astype(F32) + rows).astype(BF)


def placed_heads(place, offsets, bulk, deep):
    whole = pl.BlockSpec(memory_space=pltpu.VMEM)
    scalars = pl.BlockSpec(memory_space=pltpu.SMEM)
    return pl.pallas_call(
        place_body,
        out_shape=jax.ShapeDtypeStruct((ROWS, HEADS * DH), BF),
        in_specs=[scalars, scalars] + [whole] * 8,
        out_specs=whole,
        compiler_params=pltpu.CompilerParams(vmem_limit_bytes=VMEM_BYTES),
        cost_estimate=pl.CostEstimate(
            flops=HEADS * 2 * ROWS * DEEP * DH,
            bytes_accessed=2 * ROWS * HEADS * DH * 2,
            transcendentals=0,
        ),
        name="place",
    )(place, offsets, *bulk, *deep)


def halves(value, pieces):
    part = value.shape[1] // pieces
    return [value[:, k * part : k * part + part // 2] for k in range(pieces)]


def swap_pairs(value):
    return jnp.concatenate([value[2:], value[:2]], axis=0)


def half_slots(value, core):
    return jnp.where(core == 0, value[0::2], value[1::2])


def shards(tokens, qkv_weight, offsets):
    inner = lax.axis_index("inner").astype(I32)
    core = lax.axis_index("outer").astype(I32) & 1
    place = jnp.stack([inner, core])
    depth, width = qkv_weight.shape
    half, chunk = ROWS // 2, depth // 4
    upper, lower = tokens[:half], tokens[half:]

    y_upper = flipped(upper, 0, 2)
    z_lower = flipped(lower, 0, 1)
    chunks = [
        lax.dynamic_slice(qkv_weight, ((2 * core + k) * chunk, 0), (chunk, width)) for k in range(2)
    ]
    got = [flipped(piece, 0, 6) for piece in chunks]
    y_lower = flipped(lower, 0, 2)
    z_upper = flipped(upper, 0, 1)
    (qkv,) = project(place, offsets, [tokens], [qkv_weight], [[(0, (0,))]], 0, None, False)
    y_upper, z_lower, got[0], qkv = lax.optimization_barrier((y_upper, z_lower, got[0], qkv))
    d_upper = flipped(y_upper, 0, 1)
    d_lower = flipped(z_lower, 0, 2)
    rest = [flipped(got[0], 1, 0)]
    slabs = [z_upper, z_lower, y_upper, y_lower]
    (qkv,) = project(
        place, offsets, slabs, [qkv_weight], [[(1, (0, 1)), (2, (2, 3))]], 0, qkv, False
    )
    got[1], d_upper, d_lower, qkv = lax.optimization_barrier((got[1], d_upper, d_lower, qkv))
    rest.append(flipped(got[1], 1, 0))
    slabs = [d_upper, d_lower]
    (qkv,) = project(place, offsets, slabs, [qkv_weight], [[(3, (0, 1))]], 0, qkv, False)
    slabs = [tokens, z_upper, z_lower, y_upper, y_lower, d_upper, d_lower]
    qkv, deep_q, deep_kv = project(
        place,
        offsets,
        slabs,
        got + rest,
        [[(0, (0,)), (1, (1, 2))], [(2, (3, 4)), (3, (5, 6))]],
        2,
        qkv,
        True,
    )

    other3 = flipped(swap_pairs(deep_kv), 0, 6)
    found = near(place, offsets, qkv, 0, 2, ())
    kept = jnp.concatenate(halves(deep_kv, 1) + halves(other3, 1), axis=1)
    kept, found = lax.optimization_barrier((kept, found))
    other4 = flipped(kept, 1, 0)
    kept, other, pieces = half_slots(kept, core), half_slots(other4, core), 2
    mine, their = [], []
    for level in range(1, 4):
        kept = jnp.concatenate(halves(kept, pieces) + halves(other, pieces), axis=1)
        pieces *= 2
        if level == 2:
            *bulk, state = near(place, offsets, qkv, 2, 2, found)
            kept, bulk, state = lax.optimization_barrier((kept, bulk, state))
        if level == 3:
            bulk = [bulk[0]] + [flipped(bulk[m], 0, m) for m in range(1, SLABS)]
            done, state = middle(deep_q, state, deep_kv, other3, other4)
            kept, done, state = lax.optimization_barrier((kept, done, state))
        other = flipped(kept, 1 << level, 0)
        mine.append(other)
        their.append(flipped(other, 1, 0))
    deep = far(place, deep_q, state, done, mine, their)
    deep = [deep[0]] + [flipped(deep[m], 0, m) for m in range(1, SLABS)]
    return placed_heads(place, offsets, bulk, deep)


def solution(mesh):
    placed = (P(("outer", "inner"), None), P(None, "inner"), P())
    return jax.shard_map(
        shards, mesh=mesh, in_specs=placed, out_specs=P(("outer", "inner"), None), check_vma=False
    )
```

```python
import math

import jax
import jax.numpy as jnp
from jax import lax
from jax.experimental import pallas as pl
from jax.experimental.pallas import tpu as pltpu
from jax.sharding import PartitionSpec as P


HEADS = 16
DH = 128
ROWS = 256
DEEP = 32
SLABS = 4
SLOTS = 4
DROWS = SLABS * DEEP
BF = jnp.bfloat16
F32 = jnp.float32
I32 = jnp.int32
VMEM_BYTES = 24 * 1024 * 1024
LOW = -1e30


def flipped(value, o_mask, i_mask):
    inner = lax.axis_size("inner")
    count = inner * lax.axis_size("outer")
    mask = o_mask * inner + i_mask
    return lax.ppermute(value, ("outer", "inner"), [(f, f ^ mask) for f in range(count)])


def head_of(place_ref, m, slot):
    shard = place_ref[0] ^ m ^ (6 * (slot >> 1))
    return 2 * shard + (slot & 1)


def position_of(row, offset):
    index = row >> 1
    reverse = jnp.zeros_like(index)
    for bit in range(7):
        reverse = reverse | (((index >> bit) & 1) << (6 - bit))
    return ((row & 1) << 7) | (reverse ^ (offset & 127))


def to_order(offset):
    row = lax.broadcasted_iota(I32, (ROWS, 1), 0)
    column = lax.broadcasted_iota(I32, (ROWS, ROWS), 1)
    return jnp.where(position_of(row, offset) == column, 1.0, 0.0).astype(BF)


def from_order(offset, count):
    row = lax.broadcasted_iota(I32, (ROWS, count), 0)
    column = lax.broadcasted_iota(I32, (1, count), 1)
    return jnp.where(position_of(column, offset) == row, 1.0, 0.0).astype(BF)


def project_body(groups, n_x, n_w, first_slot, last_deep, *refs):
    place_ref, offsets_ref = refs[:2]
    xs, ws = refs[2 : 2 + n_x], refs[2 + n_x : 2 + n_x + n_w]
    qkv_ref, orders = refs[-2 - 2 * last_deep], refs[-1]
    for k in range(2):
        orders[k] = to_order(offsets_ref[head_of(place_ref, 0, first_slot + k)])
    chunk = ws[0].shape[0]
    for members in groups:
        total = None
        for index, w_ref in enumerate(ws):
            if n_w == 1:
                columns = slice(None)
            else:
                per_core = n_w // 2
                start = (place_ref[1] ^ (index // per_core)) * per_core + index % per_core
                columns = pl.ds(pl.multiple_of(start * chunk, chunk), chunk)
            rows = [xs[piece][:, columns] for _, pieces in members for piece in pieces]
            rows = rows[0] if len(rows) == 1 else jnp.concatenate(rows, axis=0)
            product = jnp.dot(rows, w_ref[...], preferred_element_type=F32)
            total = product if total is None else total + product
        total = total.astype(BF)
        for number, (m, _) in enumerate(members):
            for k in range(2):
                found = total[number * ROWS : (number + 1) * ROWS, k * 3 * DH : (k + 1) * 3 * DH]
                found = jnp.dot(orders[k], found, preferred_element_type=F32)
                qkv_ref[m, first_slot + k] = found.astype(BF)


def interleave():
    row = lax.broadcasted_iota(I32, (DROWS, DROWS), 0)
    column = lax.broadcasted_iota(I32, (DROWS, DROWS), 1)
    return jnp.where((row & 3) * DEEP + (row >> 2) == column, 1.0, 0.0).astype(BF)


def spread_body(qkv_ref, deep_q_ref, low_ref, high_ref, low_sent_ref, high_sent_ref):
    half = DROWS // 2
    for slot in range(SLOTS):
        rows = jnp.concatenate([qkv_ref[m, slot, :DEEP] for m in range(SLABS)], axis=0)
        rows = jnp.dot(interleave(), rows, preferred_element_type=F32).astype(BF)
        deep_q_ref[slot] = rows[:, :DH]
        low_ref[slot], high_ref[slot] = rows[:half, DH:], rows[half:, DH:]
        low_sent_ref[slot ^ 2], high_sent_ref[slot ^ 2] = rows[:half, DH:], rows[half:, DH:]


def project(place, offsets, xs, ws, groups, first_slot, carried, last_deep):
    whole = pl.BlockSpec(memory_space=pltpu.VMEM)
    scalars = pl.BlockSpec(memory_space=pltpu.SMEM)
    out_shape = [jax.ShapeDtypeStruct((SLABS, SLOTS, ROWS, 3 * DH), BF)]
    scratch = [pltpu.VMEM((2, ROWS, ROWS), BF)]
    if last_deep:
        out_shape += [
            jax.ShapeDtypeStruct((SLOTS, DROWS, DH), BF),
        ] + [jax.ShapeDtypeStruct((SLOTS, DROWS // 2, 2 * DH), BF) for _ in range(4)]
    extra = [] if carried is None else [carried]

    def body(*refs):
        if not last_deep:
            project_body(groups, len(xs), len(ws), first_slot, 0, *refs)
            return
        *front, qkv_ref, deep_q_ref, low, high, low_sent, high_sent, orders = refs
        project_body(groups, len(xs), len(ws), first_slot, 0, *front, qkv_ref, orders)
        spread_body(qkv_ref, deep_q_ref, low, high, low_sent, high_sent)

    slabs = sum(len(members) for members in groups)
    depth, width = xs[0].shape[1], ws[0].shape[1]
    return pl.pallas_call(
        body,
        out_shape=out_shape,
        in_specs=[scalars, scalars] + [whole] * (len(xs) + len(ws) + len(extra)),
        out_specs=[whole] * len(out_shape),
        scratch_shapes=scratch,
        input_output_aliases={2 + len(xs) + len(ws): 0} if extra else {},
        compiler_params=pltpu.CompilerParams(vmem_limit_bytes=VMEM_BYTES),
        cost_estimate=pl.CostEstimate(
            flops=slabs * 2 * ROWS * width * (depth + ROWS),
            bytes_accessed=slabs * ROWS * depth * 2 + depth * width * 2,
            transcendentals=0,
        ),
        name="project",
    )(place, offsets, *xs, *ws, *extra)


def scores_of(q, k):
    scores = lax.dot_general(q, k, (((1,), (1,)), ((), ())), preferred_element_type=F32)
    return scores * (1.0 / math.sqrt(DH))


def weigh(scores, top, v, count):
    exponent = jnp.exp(scores - top)
    if count is not None:
        exponent = exponent * count
    total = jnp.sum(exponent, axis=1, keepdims=True)
    return total, jnp.dot(exponent.astype(BF), v, preferred_element_type=F32)


def near_body(base, heads, n_extra, place_ref, offsets_ref, qkv_ref, *refs):
    *outs, state_ref = refs[n_extra:]

    @pl.loop(0, heads)
    def _(j):
        slot = base + j
        back = from_order(offsets_ref[head_of(place_ref, 0, slot)], ROWS)

        def rows_of(members, count):
            parts = []
            for part in range(3):
                pieces = [qkv_ref[m, slot, :count, part * DH : (part + 1) * DH] for m in members]
                parts.append(pieces[0] if len(pieces) == 1 else jnp.concatenate(pieces, axis=0))
            return parts

        sets = [rows_of((m,), ROWS) for m in range(SLABS)]
        sets += [rows_of((0, 1), ROWS // 2), rows_of((2, 3), ROWS // 2), rows_of(range(SLABS), ROWS // 4)]
        scores = [scores_of(q, k) for q, k, _ in sets]
        wide = [jnp.maximum(score[:, :DH], score[:, DH:]) for score in scores]
        tops = []
        for m in range(SLABS):
            pair = wide[4 + m // 2][m % 2 * 128 : m % 2 * 128 + 128]
            four = wide[6][m * 64 : m * 64 + 64]
            first = jnp.maximum(wide[m][:64], jnp.maximum(pair[:64], four))
            second = jnp.maximum(wide[m][64:128], pair[64:])
            top = jnp.concatenate([first, second, wide[m][128:]], axis=0)
            tops.append(jnp.max(top, axis=1, keepdims=True))
        tops += [jnp.concatenate([top[:128] for top in tops[2 * k : 2 * k + 2]], axis=0) for k in range(2)]
        tops.append(jnp.concatenate([top[:64] for top in tops[:SLABS]], axis=0))
        found = [weigh(scores[k], tops[k], sets[k][2], None) for k in range(7)]
        for m in range(SLABS):
            sums = []
            for part in range(2):
                dense, four = found[m][part], found[6][part][m * 64 : m * 64 + 64]
                pair = found[4 + m // 2][part][m % 2 * 128 : m % 2 * 128 + 128]
                sums.append((dense[:64] + pair[:64] + four, dense[64:128] + pair[64:], dense[128:]))
            for part, value in enumerate((tops[m], sums[0][0], sums[1][0])):
                state_ref[slot, part, pl.ds(m, DEEP, stride=SLABS), :] = jnp.broadcast_to(
                    value[:DEEP], (DEEP, DH)
                )
            done = jnp.concatenate(
                [jnp.zeros((DEEP, DH), F32), sums[1][0][DEEP:] / sums[0][0][DEEP:]]
                + [sums[1][k] / sums[0][k] for k in (1, 2)],
                axis=0,
            ).astype(BF)
            outs[m][slot] = jnp.dot(back, done, preferred_element_type=F32).astype(BF)


def near(place, offsets, qkv, base, heads, carried):
    whole = pl.BlockSpec(memory_space=pltpu.VMEM)
    scalars = pl.BlockSpec(memory_space=pltpu.SMEM)
    return pl.pallas_call(
        lambda *refs: near_body(base, heads, len(carried), *refs),
        out_shape=tuple(jax.ShapeDtypeStruct((SLOTS, ROWS, DH), BF) for _ in range(SLABS))
        + (jax.ShapeDtypeStruct((SLOTS, 3, DROWS, DH), F32),),
        in_specs=[scalars, scalars] + [whole] * (1 + len(carried)),
        out_specs=[whole] * 5,
        input_output_aliases={3 + k: k for k in range(len(carried))},
        compiler_params=pltpu.CompilerParams(vmem_limit_bytes=VMEM_BYTES),
        cost_estimate=pl.CostEstimate(
            flops=heads * 7 * 4 * ROWS * ROWS * DH,
            bytes_accessed=heads * SLABS * ROWS * 4 * DH * 2,
            transcendentals=heads * 7 * ROWS * ROWS,
        ),
        name="near",
    )(place, offsets, qkv, *carried)


def level_of(row):
    level = jnp.full_like(row, 3)
    for deeper in range(4):
        level = level + jnp.where(row < (64 >> deeper), 1, 0)
    return level


def count_of(rows, pieces, piece, lowest):
    query = level_of(lax.broadcasted_iota(I32, (rows, 1), 0))
    key = level_of(lax.broadcasted_iota(I32, (1, pieces * piece), 1) & (piece - 1))
    return jnp.maximum(jnp.minimum(query, key) - (lowest - 1), 0).astype(F32)


def join(state, scores, counts, values):
    old_top, old_total, old_mixed = state
    masked = [jnp.where(count > 0, score, LOW) for score, count in zip(scores, counts)]
    top = old_top
    for score in masked:
        top = jnp.maximum(top, jnp.max(score, axis=1, keepdims=True))
    scale = jnp.exp(old_top - top)
    total, mixed = old_total * scale, old_mixed * scale
    for score, count, value in zip(masked, counts, values):
        more_total, more_mixed = weigh(score, top, value, count)
        total, mixed = total + more_total, mixed + more_mixed
    return top, total, mixed


def middle_body(q_ref, near_ref, own_ref, other_ref, core_ref, done_ref, state_ref):
    for slot in range(SLOTS):
        state = tuple(near_ref[slot, part] for part in range(3))
        state = (state[0][:, :1], state[1][:, :1], state[2])
        keys = [own_ref[slot, :, :DH], other_ref[slot, :, :DH], core_ref[slot, :, :DH]]
        values = [own_ref[slot, :, DH:], other_ref[slot, :, DH:], core_ref[slot, :, DH:]]
        scores = [scores_of(q_ref[slot], key) for key in keys]
        counts = [count_of(DROWS, 1, DROWS, 3), count_of(DROWS, 1, DROWS, 3), count_of(DROWS, 2, 64, 4)]
        top, total, mixed = join(state, scores, counts, values)
        done_ref[slot] = mixed[DEEP:] / total[DEEP:]
        for part, value in enumerate((top, total, mixed)):
            state_ref[slot, part] = jnp.broadcast_to(value[:DEEP], (DEEP, DH))


def middle(deep_q, state, own, other, core):
    whole = pl.BlockSpec(memory_space=pltpu.VMEM)
    return pl.pallas_call(
        middle_body,
        out_shape=(
            jax.ShapeDtypeStruct((SLOTS, DROWS - DEEP, DH), F32),
            jax.ShapeDtypeStruct((SLOTS, 3, DEEP, DH), F32),
        ),
        in_specs=[whole] * 5,
        out_specs=[whole] * 2,
        compiler_params=pltpu.CompilerParams(vmem_limit_bytes=VMEM_BYTES),
        cost_estimate=pl.CostEstimate(
            flops=SLOTS * 4 * DROWS * 3 * DROWS * DH,
            bytes_accessed=SLOTS * DROWS * 10 * DH * 2,
            transcendentals=SLOTS * DROWS * 3 * DROWS,
        ),
        name="middle",
    )(deep_q, state, own, other, core)


def far_body(place_ref, q_ref, state_ref, done_ref, mine5, mine6, mine7, their5, their6, their7, *rest):
    outs, spread = rest[:SLABS], rest[SLABS]
    core = place_ref[1]
    for slot in range(SLOTS):
        state = tuple(state_ref[slot, part] for part in range(3))
        state = (state[0][:, :1], state[1][:, :1], state[2])
        keys, values = [], []
        for mine, their in ((mine5, their5), (mine6, their6), (mine7, their7)):
            found = jnp.where(core == slot % 2, mine[slot // 2], their[slot // 2])
            keys.append(found[:, :DH])
            values.append(found[:, DH:])
        scores = [scores_of(q_ref[slot, :DEEP], key) for key in keys]
        counts = [count_of(DEEP, 4, 32, 5), count_of(DEEP, 8, 16, 6), count_of(DEEP, 16, 8, 7)]
        _, total, mixed = join(state, scores, counts, values)
        spread[slot, :DEEP] = mixed / total
        spread[slot, DEEP:] = done_ref[slot]
        for m in range(SLABS):
            outs[m][slot] = spread[slot, pl.ds(m, DEEP, stride=SLABS), :].astype(BF)


def far(place, deep_q, state, done, mine, their):
    whole = pl.BlockSpec(memory_space=pltpu.VMEM)
    return pl.pallas_call(
        far_body,
        out_shape=tuple(jax.ShapeDtypeStruct((SLOTS, DEEP, DH), BF) for _ in range(SLABS)),
        in_specs=[pl.BlockSpec(memory_space=pltpu.SMEM)] + [whole] * 9,
        out_specs=[whole] * SLABS,
        scratch_shapes=[pltpu.VMEM((SLOTS, DROWS, DH), F32)],
        compiler_params=pltpu.CompilerParams(vmem_limit_bytes=VMEM_BYTES),
        cost_estimate=pl.CostEstimate(
            flops=SLOTS * 4 * DEEP * 3 * DROWS * DH,
            bytes_accessed=SLOTS * DROWS * 8 * DH * 2,
            transcendentals=SLOTS * DEEP * 3 * DROWS,
        ),
        name="far",
    )(place, deep_q, state, done, *mine, *their)


def place_body(place_ref, offsets_ref, *refs):
    bulk, deep, out_ref = refs[:4], refs[4:8], refs[8]
    for m in range(SLABS):
        for slot in range(SLOTS):
            head = head_of(place_ref, m, slot)
            back = from_order(offsets_ref[head], DEEP)
            rows = jnp.dot(back, deep[m][slot], preferred_element_type=F32)
            column = pl.multiple_of(head * DH, DH)
            early = bulk[m][slot]
            out_ref[:, pl.ds(column, DH)] = (early.astype(F32) + rows).astype(BF)


def placed_heads(place, offsets, bulk, deep):
    whole = pl.BlockSpec(memory_space=pltpu.VMEM)
    scalars = pl.BlockSpec(memory_space=pltpu.SMEM)
    return pl.pallas_call(
        place_body,
        out_shape=jax.ShapeDtypeStruct((ROWS, HEADS * DH), BF),
        in_specs=[scalars, scalars] + [whole] * 8,
        out_specs=whole,
        compiler_params=pltpu.CompilerParams(vmem_limit_bytes=VMEM_BYTES),
        cost_estimate=pl.CostEstimate(
            flops=HEADS * 2 * ROWS * DEEP * DH,
            bytes_accessed=2 * ROWS * HEADS * DH * 2,
            transcendentals=0,
        ),
        name="place",
    )(place, offsets, *bulk, *deep)


def halves(value, pieces):
    part = value.shape[1] // pieces
    return [value[:, k * part : k * part + part // 2] for k in range(pieces)]


def half_slots(value, core):
    return jnp.where(core == 0, value[0::2], value[1::2])


def shards(tokens, qkv_weight, offsets):
    inner = lax.axis_index("inner").astype(I32)
    core = lax.axis_index("outer").astype(I32) & 1
    place = jnp.stack([inner, core])
    depth, width = qkv_weight.shape
    half, chunk = ROWS // 2, depth // 4
    upper, lower = tokens[:half], tokens[half:]

    y_upper = flipped(upper, 0, 2)
    z_lower = flipped(lower, 0, 1)
    chunks = [
        lax.dynamic_slice(qkv_weight, ((2 * core + k) * chunk, 0), (chunk, width)) for k in range(2)
    ]
    got = [flipped(piece, 0, 6) for piece in chunks]
    y_lower = flipped(lower, 0, 2)
    z_upper = flipped(upper, 0, 1)
    (qkv,) = project(place, offsets, [tokens], [qkv_weight], [[(0, (0,))]], 0, None, False)
    y_upper, z_lower, got[0], qkv = lax.optimization_barrier((y_upper, z_lower, got[0], qkv))
    d_upper = flipped(y_upper, 0, 1)
    d_lower = flipped(z_lower, 0, 2)
    rest = [flipped(got[0], 1, 0)]
    slabs = [z_upper, z_lower, y_upper, y_lower]
    (qkv,) = project(
        place, offsets, slabs, [qkv_weight], [[(1, (0, 1)), (2, (2, 3))]], 0, qkv, False
    )
    got[1], d_upper, d_lower, qkv = lax.optimization_barrier((got[1], d_upper, d_lower, qkv))
    rest.append(flipped(got[1], 1, 0))
    slabs = [d_upper, d_lower]
    (qkv,) = project(place, offsets, slabs, [qkv_weight], [[(3, (0, 1))]], 0, qkv, False)
    slabs = [tokens, z_upper, z_lower, y_upper, y_lower, d_upper, d_lower]
    qkv, deep_q, low, high, low_sent, high_sent = project(
        place,
        offsets,
        slabs,
        got + rest,
        [[(0, (0,)), (1, (1, 2))], [(2, (3, 4)), (3, (5, 6))]],
        2,
        qkv,
        True,
    )

    low_other = flipped(low_sent, 0, 6)
    found = near(place, offsets, qkv, 0, 2, ())
    kept = jnp.concatenate([low, low_other], axis=1)
    kept, found = lax.optimization_barrier((kept, found))
    other4 = flipped(kept, 1, 0)
    other4, found, high_sent = lax.optimization_barrier((other4, found, high_sent))
    high_other = flipped(high_sent, 0, 6)
    kept, other, pieces = half_slots(kept, core), half_slots(other4, core), 2
    mine, their = [], []
    for level in range(1, 4):
        kept = jnp.concatenate(halves(kept, pieces) + halves(other, pieces), axis=1)
        pieces *= 2
        if level == 2:
            *bulk, state = near(place, offsets, qkv, 2, 2, found)
            kept, bulk, state = lax.optimization_barrier((kept, bulk, state))
        if level == 3:
            bulk = [bulk[0]] + [flipped(bulk[m], 0, m) for m in range(1, SLABS)]
            deep_kv = jnp.concatenate([low, high], axis=1)
            other3 = jnp.concatenate([low_other, high_other], axis=1)
            done, state = middle(deep_q, state, deep_kv, other3, other4)
            kept, done, state = lax.optimization_barrier((kept, done, state))
        other = flipped(kept, 1 << level, 0)
        if level == 3:
            other, bulk[1], bulk[2] = lax.optimization_barrier((other, bulk[1], bulk[2]))
        mine.append(other)
        their.append(flipped(other, 1, 0))
    deep = far(place, deep_q, state, done, mine, their)
    deep = [deep[0]] + [flipped(deep[m], 0, m) for m in range(1, SLABS)]
    return placed_heads(place, offsets, bulk, deep)


def solution(mesh):
    placed = (P(("outer", "inner"), None), P(None, "inner"), P())
    return jax.shard_map(
        shards, mesh=mesh, in_specs=placed, out_specs=P(("outer", "inner"), None), check_vma=False
    )
```

```python
import math

import jax
import jax.numpy as jnp
from jax import lax
from jax.experimental import pallas as pl
from jax.experimental.pallas import tpu as pltpu
from jax.sharding import PartitionSpec as P


HEADS = 16
DH = 128
ROWS = 256
DEEP = 32
SLABS = 4
SLOTS = 4
DROWS = SLABS * DEEP
BF = jnp.bfloat16
F32 = jnp.float32
I32 = jnp.int32
VMEM_BYTES = 24 * 1024 * 1024
LOW = -1e30


def flipped(value, o_mask, i_mask):
    inner = lax.axis_size("inner")
    count = inner * lax.axis_size("outer")
    mask = o_mask * inner + i_mask
    return lax.ppermute(value, ("outer", "inner"), [(f, f ^ mask) for f in range(count)])


def head_of(place_ref, m, slot):
    shard = place_ref[0] ^ m ^ (6 * (slot >> 1))
    return 2 * shard + (slot & 1)


def position_of(row, offset):
    index = row >> 1
    reverse = jnp.zeros_like(index)
    for bit in range(7):
        reverse = reverse | (((index >> bit) & 1) << (6 - bit))
    return ((row & 1) << 7) | (reverse ^ (offset & 127))


def to_order(offset):
    row = lax.broadcasted_iota(I32, (ROWS, 1), 0)
    column = lax.broadcasted_iota(I32, (ROWS, ROWS), 1)
    return jnp.where(position_of(row, offset) == column, 1.0, 0.0).astype(BF)


def from_order(offset, count):
    row = lax.broadcasted_iota(I32, (ROWS, count), 0)
    column = lax.broadcasted_iota(I32, (1, count), 1)
    return jnp.where(position_of(column, offset) == row, 1.0, 0.0).astype(BF)


def project_body(groups, n_x, n_w, first_slot, last_deep, *refs):
    place_ref, offsets_ref = refs[:2]
    xs, ws = refs[2 : 2 + n_x], refs[2 + n_x : 2 + n_x + n_w]
    qkv_ref, orders = refs[-2 - 2 * last_deep], refs[-1]
    for k in range(2):
        orders[k] = to_order(offsets_ref[head_of(place_ref, 0, first_slot + k)])
    chunk = ws[0].shape[0]
    for members in groups:
        total = None
        for index, w_ref in enumerate(ws):
            if n_w == 1:
                columns = slice(None)
            else:
                per_core = n_w // 2
                start = (place_ref[1] ^ (index // per_core)) * per_core + index % per_core
                columns = pl.ds(pl.multiple_of(start * chunk, chunk), chunk)
            rows = [xs[piece][:, columns] for _, pieces in members for piece in pieces]
            rows = rows[0] if len(rows) == 1 else jnp.concatenate(rows, axis=0)
            product = jnp.dot(rows, w_ref[...], preferred_element_type=F32)
            total = product if total is None else total + product
        total = total.astype(BF)
        for number, (m, _) in enumerate(members):
            for k in range(2):
                found = total[number * ROWS : (number + 1) * ROWS, k * 3 * DH : (k + 1) * 3 * DH]
                found = jnp.dot(orders[k], found, preferred_element_type=F32)
                qkv_ref[m, first_slot + k] = found.astype(BF)


def interleave():
    row = lax.broadcasted_iota(I32, (DROWS, DROWS), 0)
    column = lax.broadcasted_iota(I32, (DROWS, DROWS), 1)
    return jnp.where((row & 3) * DEEP + (row >> 2) == column, 1.0, 0.0).astype(BF)


def spread_body(qkv_ref, deep_q_ref, low_ref, high_ref, low_sent_ref, high_sent_ref):
    half = DROWS // 2
    for slot in range(SLOTS):
        rows = jnp.concatenate([qkv_ref[m, slot, :DEEP] for m in range(SLABS)], axis=0)
        rows = jnp.dot(interleave(), rows, preferred_element_type=F32).astype(BF)
        deep_q_ref[slot] = rows[:, :DH]
        low_ref[slot], high_ref[slot] = rows[:half, DH:], rows[half:, DH:]
        low_sent_ref[slot ^ 2], high_sent_ref[slot ^ 2] = rows[:half, DH:], rows[half:, DH:]


def project(place, offsets, xs, ws, groups, first_slot, carried, last_deep):
    whole = pl.BlockSpec(memory_space=pltpu.VMEM)
    scalars = pl.BlockSpec(memory_space=pltpu.SMEM)
    out_shape = [jax.ShapeDtypeStruct((SLABS, SLOTS, ROWS, 3 * DH), BF)]
    scratch = [pltpu.VMEM((2, ROWS, ROWS), BF)]
    if last_deep:
        out_shape += [
            jax.ShapeDtypeStruct((SLOTS, DROWS, DH), BF),
        ] + [jax.ShapeDtypeStruct((SLOTS, DROWS // 2, 2 * DH), BF) for _ in range(4)]
    extra = [] if carried is None else [carried]

    def body(*refs):
        if not last_deep:
            project_body(groups, len(xs), len(ws), first_slot, 0, *refs)
            return
        *front, qkv_ref, deep_q_ref, low, high, low_sent, high_sent, orders = refs
        project_body(groups, len(xs), len(ws), first_slot, 0, *front, qkv_ref, orders)
        spread_body(qkv_ref, deep_q_ref, low, high, low_sent, high_sent)

    slabs = sum(len(members) for members in groups)
    depth, width = xs[0].shape[1], ws[0].shape[1]
    return pl.pallas_call(
        body,
        out_shape=out_shape,
        in_specs=[scalars, scalars] + [whole] * (len(xs) + len(ws) + len(extra)),
        out_specs=[whole] * len(out_shape),
        scratch_shapes=scratch,
        input_output_aliases={2 + len(xs) + len(ws): 0} if extra else {},
        compiler_params=pltpu.CompilerParams(vmem_limit_bytes=VMEM_BYTES),
        cost_estimate=pl.CostEstimate(
            flops=slabs * 2 * ROWS * width * (depth + ROWS),
            bytes_accessed=slabs * ROWS * depth * 2 + depth * width * 2,
            transcendentals=0,
        ),
        name="project",
    )(place, offsets, *xs, *ws, *extra)


def scores_of(q, k):
    scores = lax.dot_general(q, k, (((1,), (1,)), ((), ())), preferred_element_type=F32)
    return scores * (1.0 / math.sqrt(DH))


def weigh(scores, top, v, count):
    exponent = jnp.exp(scores - top)
    if count is not None:
        exponent = exponent * count
    total = jnp.sum(exponent, axis=1, keepdims=True)
    return total, jnp.dot(exponent.astype(BF), v, preferred_element_type=F32)


def near_body(base, heads, n_extra, place_ref, offsets_ref, qkv_ref, *refs):
    *outs, state_ref = refs[n_extra:]

    @pl.loop(0, heads)
    def _(j):
        slot = base + j
        back = from_order(offsets_ref[head_of(place_ref, 0, slot)], ROWS)

        def rows_of(members, count):
            parts = []
            for part in range(3):
                pieces = [qkv_ref[m, slot, :count, part * DH : (part + 1) * DH] for m in members]
                parts.append(pieces[0] if len(pieces) == 1 else jnp.concatenate(pieces, axis=0))
            return parts

        sets = [rows_of((m,), ROWS) for m in range(SLABS)]
        sets += [rows_of((0, 1), ROWS // 2), rows_of((2, 3), ROWS // 2), rows_of(range(SLABS), ROWS // 4)]
        scores = [scores_of(q, k) for q, k, _ in sets]
        wide = [jnp.maximum(score[:, :DH], score[:, DH:]) for score in scores]
        tops = []
        for m in range(SLABS):
            pair = wide[4 + m // 2][m % 2 * 128 : m % 2 * 128 + 128]
            four = wide[6][m * 64 : m * 64 + 64]
            first = jnp.maximum(wide[m][:64], jnp.maximum(pair[:64], four))
            second = jnp.maximum(wide[m][64:128], pair[64:])
            top = jnp.concatenate([first, second, wide[m][128:]], axis=0)
            tops.append(jnp.max(top, axis=1, keepdims=True))
        tops += [jnp.concatenate([top[:128] for top in tops[2 * k : 2 * k + 2]], axis=0) for k in range(2)]
        tops.append(jnp.concatenate([top[:64] for top in tops[:SLABS]], axis=0))
        found = [weigh(scores[k], tops[k], sets[k][2], None) for k in range(7)]
        for m in range(SLABS):
            sums = []
            for part in range(2):
                dense, four = found[m][part], found[6][part][m * 64 : m * 64 + 64]
                pair = found[4 + m // 2][part][m % 2 * 128 : m % 2 * 128 + 128]
                sums.append((dense[:64] + pair[:64] + four, dense[64:128] + pair[64:], dense[128:]))
            for part, value in enumerate((tops[m], sums[0][0], sums[1][0])):
                state_ref[slot, part, pl.ds(m, DEEP, stride=SLABS), :] = jnp.broadcast_to(
                    value[:DEEP], (DEEP, DH)
                )
            done = jnp.concatenate(
                [jnp.zeros((DEEP, DH), F32), sums[1][0][DEEP:] / sums[0][0][DEEP:]]
                + [sums[1][k] / sums[0][k] for k in (1, 2)],
                axis=0,
            ).astype(BF)
            outs[m][slot] = jnp.dot(back, done, preferred_element_type=F32).astype(BF)


def near(place, offsets, qkv, base, heads, carried):
    whole = pl.BlockSpec(memory_space=pltpu.VMEM)
    scalars = pl.BlockSpec(memory_space=pltpu.SMEM)
    return pl.pallas_call(
        lambda *refs: near_body(base, heads, len(carried), *refs),
        out_shape=tuple(jax.ShapeDtypeStruct((SLOTS, ROWS, DH), BF) for _ in range(SLABS))
        + (jax.ShapeDtypeStruct((SLOTS, 3, DROWS, DH), F32),),
        in_specs=[scalars, scalars] + [whole] * (1 + len(carried)),
        out_specs=[whole] * 5,
        input_output_aliases={3 + k: k for k in range(len(carried))},
        compiler_params=pltpu.CompilerParams(vmem_limit_bytes=VMEM_BYTES),
        cost_estimate=pl.CostEstimate(
            flops=heads * 7 * 4 * ROWS * ROWS * DH,
            bytes_accessed=heads * SLABS * ROWS * 4 * DH * 2,
            transcendentals=heads * 7 * ROWS * ROWS,
        ),
        name="near",
    )(place, offsets, qkv, *carried)


def level_of(row):
    level = jnp.full_like(row, 3)
    for deeper in range(4):
        level = level + jnp.where(row < (64 >> deeper), 1, 0)
    return level


def count_of(rows, pieces, piece, lowest):
    query = level_of(lax.broadcasted_iota(I32, (rows, 1), 0))
    key = level_of(lax.broadcasted_iota(I32, (1, pieces * piece), 1) & (piece - 1))
    return jnp.maximum(jnp.minimum(query, key) - (lowest - 1), 0).astype(F32)


def join(state, scores, counts, values):
    old_top, old_total, old_mixed = state
    masked = [jnp.where(count > 0, score, LOW) for score, count in zip(scores, counts)]
    top = old_top
    for score in masked:
        top = jnp.maximum(top, jnp.max(score, axis=1, keepdims=True))
    scale = jnp.exp(old_top - top)
    total, mixed = old_total * scale, old_mixed * scale
    for score, count, value in zip(masked, counts, values):
        more_total, more_mixed = weigh(score, top, value, count)
        total, mixed = total + more_total, mixed + more_mixed
    return top, total, mixed


def middle_body(q_ref, near_ref, own_ref, other_ref, core_ref, done_ref, state_ref):
    for slot in range(SLOTS):
        state = tuple(near_ref[slot, part] for part in range(3))
        state = (state[0][:, :1], state[1][:, :1], state[2])
        keys = [own_ref[slot, :, :DH], other_ref[slot, :, :DH], core_ref[slot, :, :DH]]
        values = [own_ref[slot, :, DH:], other_ref[slot, :, DH:], core_ref[slot, :, DH:]]
        scores = [scores_of(q_ref[slot], key) for key in keys]
        counts = [count_of(DROWS, 1, DROWS, 3), count_of(DROWS, 1, DROWS, 3), count_of(DROWS, 2, 64, 4)]
        top, total, mixed = join(state, scores, counts, values)
        done_ref[slot] = mixed[DEEP:] / total[DEEP:]
        for part, value in enumerate((top, total, mixed)):
            state_ref[slot, part] = jnp.broadcast_to(value[:DEEP], (DEEP, DH))


def middle(deep_q, state, own, other, core):
    whole = pl.BlockSpec(memory_space=pltpu.VMEM)
    return pl.pallas_call(
        middle_body,
        out_shape=(
            jax.ShapeDtypeStruct((SLOTS, DROWS - DEEP, DH), F32),
            jax.ShapeDtypeStruct((SLOTS, 3, DEEP, DH), F32),
        ),
        in_specs=[whole] * 5,
        out_specs=[whole] * 2,
        compiler_params=pltpu.CompilerParams(vmem_limit_bytes=VMEM_BYTES),
        cost_estimate=pl.CostEstimate(
            flops=SLOTS * 4 * DROWS * 3 * DROWS * DH,
            bytes_accessed=SLOTS * DROWS * 10 * DH * 2,
            transcendentals=SLOTS * DROWS * 3 * DROWS,
        ),
        name="middle",
    )(deep_q, state, own, other, core)


def far_body(place_ref, q_ref, state_ref, done_ref, mine5, mine6, mine7, their5, their6, their7, *rest):
    outs, spread = rest[:SLABS], rest[SLABS]
    core = place_ref[1]
    for slot in range(SLOTS):
        state = tuple(state_ref[slot, part] for part in range(3))
        state = (state[0][:, :1], state[1][:, :1], state[2])
        keys, values = [], []
        for mine, their in ((mine5, their5), (mine6, their6), (mine7, their7)):
            found = jnp.where(core == slot % 2, mine[slot // 2], their[slot // 2])
            keys.append(found[:, :DH])
            values.append(found[:, DH:])
        scores = [scores_of(q_ref[slot, :DEEP], key) for key in keys]
        counts = [count_of(DEEP, 4, 32, 5), count_of(DEEP, 8, 16, 6), count_of(DEEP, 16, 8, 7)]
        _, total, mixed = join(state, scores, counts, values)
        spread[slot, :DEEP] = mixed / total
        spread[slot, DEEP:] = done_ref[slot]
        for m in range(SLABS):
            outs[m][slot] = spread[slot, pl.ds(m, DEEP, stride=SLABS), :].astype(BF)


def far(place, deep_q, state, done, mine, their):
    whole = pl.BlockSpec(memory_space=pltpu.VMEM)
    return pl.pallas_call(
        far_body,
        out_shape=tuple(jax.ShapeDtypeStruct((SLOTS, DEEP, DH), BF) for _ in range(SLABS)),
        in_specs=[pl.BlockSpec(memory_space=pltpu.SMEM)] + [whole] * 9,
        out_specs=[whole] * SLABS,
        scratch_shapes=[pltpu.VMEM((SLOTS, DROWS, DH), F32)],
        compiler_params=pltpu.CompilerParams(vmem_limit_bytes=VMEM_BYTES),
        cost_estimate=pl.CostEstimate(
            flops=SLOTS * 4 * DEEP * 3 * DROWS * DH,
            bytes_accessed=SLOTS * DROWS * 8 * DH * 2,
            transcendentals=SLOTS * DEEP * 3 * DROWS,
        ),
        name="far",
    )(place, deep_q, state, done, *mine, *their)


def place_body(place_ref, offsets_ref, *refs):
    bulk, deep, out_ref = refs[:4], refs[4:8], refs[8]
    for m in range(SLABS):
        for slot in range(SLOTS):
            head = head_of(place_ref, m, slot)
            back = from_order(offsets_ref[head], DEEP)
            rows = jnp.dot(back, deep[m][slot], preferred_element_type=F32)
            column = pl.multiple_of(head * DH, DH)
            early = bulk[m][slot]
            out_ref[:, pl.ds(column, DH)] = (early.astype(F32) + rows).astype(BF)


def placed_heads(place, offsets, bulk, deep):
    whole = pl.BlockSpec(memory_space=pltpu.VMEM)
    scalars = pl.BlockSpec(memory_space=pltpu.SMEM)
    return pl.pallas_call(
        place_body,
        out_shape=jax.ShapeDtypeStruct((ROWS, HEADS * DH), BF),
        in_specs=[scalars, scalars] + [whole] * 8,
        out_specs=whole,
        compiler_params=pltpu.CompilerParams(vmem_limit_bytes=VMEM_BYTES),
        cost_estimate=pl.CostEstimate(
            flops=HEADS * 2 * ROWS * DEEP * DH,
            bytes_accessed=2 * ROWS * HEADS * DH * 2,
            transcendentals=0,
        ),
        name="place",
    )(place, offsets, *bulk, *deep)


def halves(value, pieces):
    part = value.shape[1] // pieces
    return [value[:, k * part : k * part + part // 2] for k in range(pieces)]


def half_slots(value, core):
    return jnp.where(core == 0, value[0::2], value[1::2])


def shards(tokens, qkv_weight, offsets):
    inner = lax.axis_index("inner").astype(I32)
    core = lax.axis_index("outer").astype(I32) & 1
    place = jnp.stack([inner, core])
    depth, width = qkv_weight.shape
    half, chunk = ROWS // 2, depth // 4
    upper, lower = tokens[:half], tokens[half:]

    y_upper = flipped(upper, 0, 2)
    z_lower = flipped(lower, 0, 1)
    chunks = [
        lax.dynamic_slice(qkv_weight, ((2 * core + k) * chunk, 0), (chunk, width)) for k in range(2)
    ]
    got = [flipped(piece, 0, 6) for piece in chunks]
    y_lower = flipped(lower, 0, 2)
    z_upper = flipped(upper, 0, 1)
    (qkv,) = project(place, offsets, [tokens], [qkv_weight], [[(0, (0,))]], 0, None, False)
    y_upper, z_lower, got[0], qkv = lax.optimization_barrier((y_upper, z_lower, got[0], qkv))
    d_upper = flipped(y_upper, 0, 1)
    d_lower = flipped(z_lower, 0, 2)
    rest = [flipped(got[0], 1, 0)]
    slabs = [z_upper, z_lower, y_upper, y_lower]
    (qkv,) = project(
        place, offsets, slabs, [qkv_weight], [[(1, (0, 1)), (2, (2, 3))]], 0, qkv, False
    )
    got[1], d_upper, d_lower, qkv = lax.optimization_barrier((got[1], d_upper, d_lower, qkv))
    rest.append(flipped(got[1], 1, 0))
    slabs = [d_upper, d_lower]
    (qkv,) = project(place, offsets, slabs, [qkv_weight], [[(3, (0, 1))]], 0, qkv, False)
    slabs = [tokens, z_upper, z_lower, y_upper, y_lower, d_upper, d_lower]
    qkv, deep_q, low, high, low_sent, high_sent = project(
        place,
        offsets,
        slabs,
        got + rest,
        [[(0, (0,)), (1, (1, 2))], [(2, (3, 4)), (3, (5, 6))]],
        2,
        qkv,
        True,
    )

    low_other = flipped(low_sent, 0, 6)
    found = near(place, offsets, qkv, 0, 2, ())
    low, low_other, found = lax.optimization_barrier((low, low_other, found))
    low_core = flipped(low, 1, 0)
    low_both = flipped(low_other, 1, 0)
    other4 = jnp.concatenate([low_core, low_both], axis=1)
    other4, found, high_sent = lax.optimization_barrier((other4, found, high_sent))
    high_other = flipped(high_sent, 0, 6)
    kept = jnp.concatenate([half_slots(low, core), half_slots(low_other, core)], axis=1)
    other, pieces = half_slots(other4, core), 2
    mine, their = [], []
    for level in range(1, 4):
        kept = jnp.concatenate(halves(kept, pieces) + halves(other, pieces), axis=1)
        pieces *= 2
        if level == 2:
            *bulk, state = near(place, offsets, qkv, 2, 2, found)
            kept, bulk, state = lax.optimization_barrier((kept, bulk, state))
        if level == 3:
            bulk = [bulk[0]] + [flipped(bulk[m], 0, m) for m in range(1, SLABS)]
            deep_kv = jnp.concatenate([low, high], axis=1)
            other3 = jnp.concatenate([low_other, high_other], axis=1)
            done, state = middle(deep_q, state, deep_kv, other3, other4)
            kept, done, state = lax.optimization_barrier((kept, done, state))
        other = flipped(kept, 1 << level, 0)
        if level == 3:
            other, bulk[1], bulk[2] = lax.optimization_barrier((other, bulk[1], bulk[2]))
        mine.append(other)
        their.append(flipped(other, 1, 0))
    deep = far(place, deep_q, state, done, mine, their)
    deep = [deep[0]] + [flipped(deep[m], 0, m) for m in range(1, SLABS)]
    return placed_heads(place, offsets, bulk, deep)


def solution(mesh):
    placed = (P(("outer", "inner"), None), P(None, "inner"), P())
    return jax.shard_map(
        shards, mesh=mesh, in_specs=placed, out_specs=P(("outer", "inner"), None), check_vma=False
    )
```

```python
import math

import jax
import jax.numpy as jnp
from jax import lax
from jax.experimental import pallas as pl
from jax.experimental.pallas import tpu as pltpu
from jax.sharding import PartitionSpec as P


HEADS = 16
DH = 128
ROWS = 256
DEEP = 32
SLABS = 4
SLOTS = 4
DROWS = SLABS * DEEP
BF = jnp.bfloat16
F32 = jnp.float32
I32 = jnp.int32
VMEM_BYTES = 24 * 1024 * 1024
LOW = -1e30


def flipped(value, o_mask, i_mask):
    inner = lax.axis_size("inner")
    count = inner * lax.axis_size("outer")
    mask = o_mask * inner + i_mask
    return lax.ppermute(value, ("outer", "inner"), [(f, f ^ mask) for f in range(count)])


def head_of(place_ref, m, slot):
    shard = place_ref[0] ^ m ^ (6 * (slot >> 1))
    return 2 * shard + (slot & 1)


def position_of(row, offset):
    index = row >> 1
    reverse = jnp.zeros_like(index)
    for bit in range(7):
        reverse = reverse | (((index >> bit) & 1) << (6 - bit))
    return ((row & 1) << 7) | (reverse ^ (offset & 127))


def to_order(offset):
    row = lax.broadcasted_iota(I32, (ROWS, 1), 0)
    column = lax.broadcasted_iota(I32, (ROWS, ROWS), 1)
    return jnp.where(position_of(row, offset) == column, 1.0, 0.0).astype(BF)


def from_order(offset, count):
    row = lax.broadcasted_iota(I32, (ROWS, count), 0)
    column = lax.broadcasted_iota(I32, (1, count), 1)
    return jnp.where(position_of(column, offset) == row, 1.0, 0.0).astype(BF)


def project_body(groups, n_x, n_w, first_slot, last_deep, *refs):
    place_ref, offsets_ref = refs[:2]
    xs, ws = refs[2 : 2 + n_x], refs[2 + n_x : 2 + n_x + n_w]
    qkv_ref, orders = refs[-2 - 2 * last_deep], refs[-1]
    for k in range(2):
        orders[k] = to_order(offsets_ref[head_of(place_ref, 0, first_slot + k)])
    chunk = ws[0].shape[0]
    for members in groups:
        total = None
        for index, w_ref in enumerate(ws):
            if n_w == 1:
                columns = slice(None)
            else:
                per_core = n_w // 2
                start = (place_ref[1] ^ (index // per_core)) * per_core + index % per_core
                columns = pl.ds(pl.multiple_of(start * chunk, chunk), chunk)
            rows = [xs[piece][:, columns] for _, pieces in members for piece in pieces]
            rows = rows[0] if len(rows) == 1 else jnp.concatenate(rows, axis=0)
            product = jnp.dot(rows, w_ref[...], preferred_element_type=F32)
            total = product if total is None else total + product
        total = total.astype(BF)
        for number, (m, _) in enumerate(members):
            for k in range(2):
                found = total[number * ROWS : (number + 1) * ROWS, k * 3 * DH : (k + 1) * 3 * DH]
                found = jnp.dot(orders[k], found, preferred_element_type=F32)
                qkv_ref[m, first_slot + k] = found.astype(BF)


def interleave():
    row = lax.broadcasted_iota(I32, (DROWS, DROWS), 0)
    column = lax.broadcasted_iota(I32, (DROWS, DROWS), 1)
    return jnp.where((row & 3) * DEEP + (row >> 2) == column, 1.0, 0.0).astype(BF)


def spread_body(qkv_ref, deep_q_ref, low_ref, high_ref, low_sent_ref):
    half = DROWS // 2
    for slot in range(SLOTS):
        rows = jnp.concatenate([qkv_ref[m, slot, :DEEP] for m in range(SLABS)], axis=0)
        rows = jnp.dot(interleave(), rows, preferred_element_type=F32).astype(BF)
        deep_q_ref[slot] = rows[:, :DH]
        low_ref[slot], high_ref[slot] = rows[:half, DH:], rows[half:, DH:]
        low_sent_ref[slot ^ 2] = rows[:half, DH:]


def project(place, offsets, xs, ws, groups, first_slot, carried, last_deep):
    whole = pl.BlockSpec(memory_space=pltpu.VMEM)
    scalars = pl.BlockSpec(memory_space=pltpu.SMEM)
    out_shape = [jax.ShapeDtypeStruct((SLABS, SLOTS, ROWS, 3 * DH), BF)]
    scratch = [pltpu.VMEM((2, ROWS, ROWS), BF)]
    if last_deep:
        out_shape += [
            jax.ShapeDtypeStruct((SLOTS, DROWS, DH), BF),
        ] + [jax.ShapeDtypeStruct((SLOTS, DROWS // 2, 2 * DH), BF) for _ in range(3)]
    extra = [] if carried is None else [carried]

    def body(*refs):
        if not last_deep:
            project_body(groups, len(xs), len(ws), first_slot, 0, *refs)
            return
        *front, qkv_ref, deep_q_ref, low, high, low_sent, orders = refs
        project_body(groups, len(xs), len(ws), first_slot, 0, *front, qkv_ref, orders)
        spread_body(qkv_ref, deep_q_ref, low, high, low_sent)

    slabs = sum(len(members) for members in groups)
    depth, width = xs[0].shape[1], ws[0].shape[1]
    return pl.pallas_call(
        body,
        out_shape=out_shape,
        in_specs=[scalars, scalars] + [whole] * (len(xs) + len(ws) + len(extra)),
        out_specs=[whole] * len(out_shape),
        scratch_shapes=scratch,
        input_output_aliases={2 + len(xs) + len(ws): 0} if extra else {},
        compiler_params=pltpu.CompilerParams(vmem_limit_bytes=VMEM_BYTES),
        cost_estimate=pl.CostEstimate(
            flops=slabs * 2 * ROWS * width * (depth + ROWS),
            bytes_accessed=slabs * ROWS * depth * 2 + depth * width * 2,
            transcendentals=0,
        ),
        name="project",
    )(place, offsets, *xs, *ws, *extra)


def scores_of(q, k):
    scores = lax.dot_general(q, k, (((1,), (1,)), ((), ())), preferred_element_type=F32)
    return scores * (1.0 / math.sqrt(DH))


def weigh(scores, top, v, count):
    exponent = jnp.exp(scores - top)
    if count is not None:
        exponent = exponent * count
    total = jnp.sum(exponent, axis=1, keepdims=True)
    return total, jnp.dot(exponent.astype(BF), v, preferred_element_type=F32)


def near_body(base, heads, n_extra, place_ref, offsets_ref, qkv_ref, *refs):
    *outs, state_ref = refs[n_extra:]

    @pl.loop(0, heads)
    def _(j):
        slot = base + j
        back = from_order(offsets_ref[head_of(place_ref, 0, slot)], ROWS)

        def rows_of(members, count):
            parts = []
            for part in range(3):
                pieces = [qkv_ref[m, slot, :count, part * DH : (part + 1) * DH] for m in members]
                parts.append(pieces[0] if len(pieces) == 1 else jnp.concatenate(pieces, axis=0))
            return parts

        sets = [rows_of((m,), ROWS) for m in range(SLABS)]
        sets += [rows_of((0, 1), ROWS // 2), rows_of((2, 3), ROWS // 2), rows_of(range(SLABS), ROWS // 4)]
        scores = [scores_of(q, k) for q, k, _ in sets]
        wide = [jnp.maximum(score[:, :DH], score[:, DH:]) for score in scores]
        tops = []
        for m in range(SLABS):
            pair = wide[4 + m // 2][m % 2 * 128 : m % 2 * 128 + 128]
            four = wide[6][m * 64 : m * 64 + 64]
            first = jnp.maximum(wide[m][:64], jnp.maximum(pair[:64], four))
            second = jnp.maximum(wide[m][64:128], pair[64:])
            top = jnp.concatenate([first, second, wide[m][128:]], axis=0)
            tops.append(jnp.max(top, axis=1, keepdims=True))
        tops += [jnp.concatenate([top[:128] for top in tops[2 * k : 2 * k + 2]], axis=0) for k in range(2)]
        tops.append(jnp.concatenate([top[:64] for top in tops[:SLABS]], axis=0))
        found = [weigh(scores[k], tops[k], sets[k][2], None) for k in range(7)]
        for m in range(SLABS):
            sums = []
            for part in range(2):
                dense, four = found[m][part], found[6][part][m * 64 : m * 64 + 64]
                pair = found[4 + m // 2][part][m % 2 * 128 : m % 2 * 128 + 128]
                sums.append((dense[:64] + pair[:64] + four, dense[64:128] + pair[64:], dense[128:]))
            for part, value in enumerate((tops[m], sums[0][0], sums[1][0])):
                state_ref[slot, part, pl.ds(m, DEEP, stride=SLABS), :] = jnp.broadcast_to(
                    value[:DEEP], (DEEP, DH)
                )
            done = jnp.concatenate(
                [jnp.zeros((DEEP, DH), F32), sums[1][0][DEEP:] / sums[0][0][DEEP:]]
                + [sums[1][k] / sums[0][k] for k in (1, 2)],
                axis=0,
            ).astype(BF)
            outs[m][slot] = jnp.dot(back, done, preferred_element_type=F32).astype(BF)


def near(place, offsets, qkv, base, heads, carried):
    whole = pl.BlockSpec(memory_space=pltpu.VMEM)
    scalars = pl.BlockSpec(memory_space=pltpu.SMEM)
    return pl.pallas_call(
        lambda *refs: near_body(base, heads, len(carried), *refs),
        out_shape=tuple(jax.ShapeDtypeStruct((SLOTS, ROWS, DH), BF) for _ in range(SLABS))
        + (jax.ShapeDtypeStruct((SLOTS, 3, DROWS, DH), F32),),
        in_specs=[scalars, scalars] + [whole] * (1 + len(carried)),
        out_specs=[whole] * 5,
        input_output_aliases={3 + k: k for k in range(len(carried))},
        compiler_params=pltpu.CompilerParams(vmem_limit_bytes=VMEM_BYTES),
        cost_estimate=pl.CostEstimate(
            flops=heads * 7 * 4 * ROWS * ROWS * DH,
            bytes_accessed=heads * SLABS * ROWS * 4 * DH * 2,
            transcendentals=heads * 7 * ROWS * ROWS,
        ),
        name="near",
    )(place, offsets, qkv, *carried)


def level_of(row):
    level = jnp.full_like(row, 3)
    for deeper in range(4):
        level = level + jnp.where(row < (64 >> deeper), 1, 0)
    return level


def count_of(rows, pieces, piece, lowest):
    query = level_of(lax.broadcasted_iota(I32, (rows, 1), 0))
    key = level_of(lax.broadcasted_iota(I32, (1, pieces * piece), 1) & (piece - 1))
    return jnp.maximum(jnp.minimum(query, key) - (lowest - 1), 0).astype(F32)


def join(state, scores, counts, values):
    old_top, old_total, old_mixed = state
    masked = [
        score if count is None else jnp.where(count > 0, score, LOW)
        for score, count in zip(scores, counts)
    ]
    top = old_top
    for score in masked:
        top = jnp.maximum(top, jnp.max(score, axis=1, keepdims=True))
    scale = jnp.exp(old_top - top)
    total, mixed = old_total * scale, old_mixed * scale
    for score, count, value in zip(masked, counts, values):
        more_total, more_mixed = weigh(score, top, value, count)
        total, mixed = total + more_total, mixed + more_mixed
    return top, total, mixed


def middle_body(q_ref, near_ref, *refs):
    key_refs, done_ref, state_ref = refs[:6], refs[6], refs[7]
    half = DROWS // 2
    counts = [count_of(DROWS, 1, half, 3)] * 2 + [None] * 2 + [count_of(DROWS, 1, half, 4)] * 2
    for slot in range(SLOTS):
        state = tuple(near_ref[slot, part] for part in range(3))
        state = (state[0][:, :1], state[1][:, :1], state[2])
        keys = [jnp.concatenate([ref[slot] for ref in key_refs[k : k + 2]], axis=0) for k in (0, 2, 4)]
        pairs = [
            None if counts[k] is None else jnp.concatenate(counts[k : k + 2], axis=1) for k in (0, 2, 4)
        ]
        scores = [scores_of(q_ref[slot], key[:, :DH]) for key in keys]
        top, total, mixed = join(state, scores, pairs, [key[:, DH:] for key in keys])
        done_ref[slot] = mixed[DEEP:] / total[DEEP:]
        for part, value in enumerate((top, total, mixed)):
            state_ref[slot, part] = jnp.broadcast_to(value[:DEEP], (DEEP, DH))


def middle(deep_q, state, keys):
    whole = pl.BlockSpec(memory_space=pltpu.VMEM)
    return pl.pallas_call(
        middle_body,
        out_shape=(
            jax.ShapeDtypeStruct((SLOTS, DROWS - DEEP, DH), F32),
            jax.ShapeDtypeStruct((SLOTS, 3, DEEP, DH), F32),
        ),
        in_specs=[whole] * (2 + len(keys)),
        out_specs=[whole] * 2,
        compiler_params=pltpu.CompilerParams(vmem_limit_bytes=VMEM_BYTES),
        cost_estimate=pl.CostEstimate(
            flops=SLOTS * 4 * DROWS * 3 * DROWS * DH,
            bytes_accessed=SLOTS * DROWS * 10 * DH * 2,
            transcendentals=SLOTS * DROWS * 3 * DROWS,
        ),
        name="middle",
    )(deep_q, state, *keys)


def far_body(place_ref, q_ref, state_ref, done_ref, mine5, mine6, mine7, their5, their6, their7, *rest):
    outs, spread = rest[:SLABS], rest[SLABS]
    core = place_ref[1]
    for slot in range(SLOTS):
        state = tuple(state_ref[slot, part] for part in range(3))
        state = (state[0][:, :1], state[1][:, :1], state[2])
        keys, values = [], []
        for mine, their in ((mine5, their5), (mine6, their6), (mine7, their7)):
            found = jnp.where(core == slot % 2, mine[slot // 2], their[slot // 2])
            keys.append(found[:, :DH])
            values.append(found[:, DH:])
        scores = [scores_of(q_ref[slot, :DEEP], key) for key in keys]
        counts = [count_of(DEEP, 4, 32, 5), count_of(DEEP, 8, 16, 6), count_of(DEEP, 16, 8, 7)]
        _, total, mixed = join(state, scores, counts, values)
        spread[slot, :DEEP] = mixed / total
        spread[slot, DEEP:] = done_ref[slot]
        for m in range(SLABS):
            outs[m][slot] = spread[slot, pl.ds(m, DEEP, stride=SLABS), :].astype(BF)


def far(place, deep_q, state, done, mine, their):
    whole = pl.BlockSpec(memory_space=pltpu.VMEM)
    return pl.pallas_call(
        far_body,
        out_shape=tuple(jax.ShapeDtypeStruct((SLOTS, DEEP, DH), BF) for _ in range(SLABS)),
        in_specs=[pl.BlockSpec(memory_space=pltpu.SMEM)] + [whole] * 9,
        out_specs=[whole] * SLABS,
        scratch_shapes=[pltpu.VMEM((SLOTS, DROWS, DH), F32)],
        compiler_params=pltpu.CompilerParams(vmem_limit_bytes=VMEM_BYTES),
        cost_estimate=pl.CostEstimate(
            flops=SLOTS * 4 * DEEP * 3 * DROWS * DH,
            bytes_accessed=SLOTS * DROWS * 8 * DH * 2,
            transcendentals=SLOTS * DEEP * 3 * DROWS,
        ),
        name="far",
    )(place, deep_q, state, done, *mine, *their)


def place_body(place_ref, offsets_ref, *refs):
    bulk, deep, out_ref = refs[:4], refs[4:8], refs[8]
    for m in range(SLABS):
        for slot in range(SLOTS):
            head = head_of(place_ref, m, slot)
            back = from_order(offsets_ref[head], DEEP)
            rows = jnp.dot(back, deep[m][slot], preferred_element_type=F32)
            column = pl.multiple_of(head * DH, DH)
            early = bulk[m][slot]
            out_ref[:, pl.ds(column, DH)] = (early.astype(F32) + rows).astype(BF)


def placed_heads(place, offsets, bulk, deep):
    whole = pl.BlockSpec(memory_space=pltpu.VMEM)
    scalars = pl.BlockSpec(memory_space=pltpu.SMEM)
    return pl.pallas_call(
        place_body,
        out_shape=jax.ShapeDtypeStruct((ROWS, HEADS * DH), BF),
        in_specs=[scalars, scalars] + [whole] * 8,
        out_specs=whole,
        compiler_params=pltpu.CompilerParams(vmem_limit_bytes=VMEM_BYTES),
        cost_estimate=pl.CostEstimate(
            flops=HEADS * 2 * ROWS * DEEP * DH,
            bytes_accessed=2 * ROWS * HEADS * DH * 2,
            transcendentals=0,
        ),
        name="place",
    )(place, offsets, *bulk, *deep)


def halves(value, pieces):
    part = value.shape[1] // pieces
    return [value[:, k * part : k * part + part // 2] for k in range(pieces)]


def half_slots(value, core):
    return jnp.where(core == 0, value[0::2], value[1::2])


def shards(tokens, qkv_weight, offsets):
    inner = lax.axis_index("inner").astype(I32)
    core = lax.axis_index("outer").astype(I32) & 1
    place = jnp.stack([inner, core])
    depth, width = qkv_weight.shape
    half, chunk = ROWS // 2, depth // 4
    upper, lower = tokens[:half], tokens[half:]

    y_upper = flipped(upper, 0, 2)
    z_lower = flipped(lower, 0, 1)
    chunks = [
        lax.dynamic_slice(qkv_weight, ((2 * core + k) * chunk, 0), (chunk, width)) for k in range(2)
    ]
    got = [flipped(piece, 0, 6) for piece in chunks]
    y_lower = flipped(lower, 0, 2)
    z_upper = flipped(upper, 0, 1)
    (qkv,) = project(place, offsets, [tokens], [qkv_weight], [[(0, (0,))]], 0, None, False)
    y_upper, z_lower, got[0], qkv = lax.optimization_barrier((y_upper, z_lower, got[0], qkv))
    d_upper = flipped(y_upper, 0, 1)
    d_lower = flipped(z_lower, 0, 2)
    rest = [flipped(got[0], 1, 0)]
    slabs = [z_upper, z_lower, y_upper, y_lower]
    (qkv,) = project(
        place, offsets, slabs, [qkv_weight], [[(1, (0, 1)), (2, (2, 3))]], 0, qkv, False
    )
    got[1], d_upper, d_lower, qkv = lax.optimization_barrier((got[1], d_upper, d_lower, qkv))
    rest.append(flipped(got[1], 1, 0))
    slabs = [d_upper, d_lower]
    (qkv,) = project(place, offsets, slabs, [qkv_weight], [[(3, (0, 1))]], 0, qkv, False)
    slabs = [tokens, z_upper, z_lower, y_upper, y_lower, d_upper, d_lower]
    qkv, deep_q, low, high, low_sent = project(
        place,
        offsets,
        slabs,
        got + rest,
        [[(0, (0,)), (1, (1, 2))], [(2, (3, 4)), (3, (5, 6))]],
        2,
        qkv,
        True,
    )

    low_other = flipped(low_sent, 0, 6)
    found = near(place, offsets, qkv, 0, 2, ())
    low, low_other, found = lax.optimization_barrier((low, low_other, found))
    low_core = flipped(low, 1, 0)
    low_both = flipped(low_other, 1, 0)
    low_both, found, high = lax.optimization_barrier((low_both, found, high))
    high_other = flipped(jnp.concatenate([high[2:], high[:2]], axis=0), 0, 6)
    kept = jnp.concatenate([half_slots(low, core), half_slots(low_other, core)], axis=1)
    other = jnp.concatenate([half_slots(low_core, core), half_slots(low_both, core)], axis=1)
    pieces = 2
    mine, their = [], []
    for level in range(1, 4):
        kept = jnp.concatenate(halves(kept, pieces) + halves(other, pieces), axis=1)
        pieces *= 2
        if level == 2:
            *bulk, state = near(place, offsets, qkv, 2, 2, found)
            kept, bulk, state = lax.optimization_barrier((kept, bulk, state))
        if level == 3:
            bulk = [bulk[0]] + [flipped(bulk[m], 0, m) for m in range(1, SLABS)]
            keys = (low, low_other, high, high_other, low_core, low_both)
            done, state = middle(deep_q, state, keys)
            kept, done, state = lax.optimization_barrier((kept, done, state))
        other = flipped(kept, 1 << level, 0)
        if level == 3:
            other, bulk[1], bulk[2] = lax.optimization_barrier((other, bulk[1], bulk[2]))
        mine.append(other)
        their.append(flipped(other, 1, 0))
    deep = far(place, deep_q, state, done, mine, their)
    deep = [deep[0]] + [flipped(deep[m], 0, m) for m in range(1, SLABS)]
    return placed_heads(place, offsets, bulk, deep)


def solution(mesh):
    placed = (P(("outer", "inner"), None), P(None, "inner"), P())
    return jax.shard_map(
        shards, mesh=mesh, in_specs=placed, out_specs=P(("outer", "inner"), None), check_vma=False
    )
```
